128 devices in a mesh: ctx: 16 (over x, y_hi, core), head: 8 (over z, y_lo).
Axes of the slice: x: 4, y: 4 (y_hi: 2, y_lo: 2; y = y_hi * 2 + y_lo), z: 4, core: 2. Of those that a mesh axis runs over, the one named last changes fastest.
Arguments:
- queries: bfloat16 [2, 8192, 5120], P(None, ('ctx', 'head')), may hold values from -6 to 6
- keys: bfloat16 [2, 8192, 5120], P(None, ('ctx', 'head')), may hold values from -6 to 6
- values: bfloat16 [2, 8192, 5120], P(None, ('ctx', 'head')), may hold values from -6 to 6
- rates: bfloat16 [2, 8192, 8], P(None, ('ctx', 'head')), may hold values from 0.00013065338 to 0.0013046265
- gate_fast: float32 [8, 640, 640], P('head'), may hold values from -0.25 to 0.25
- up_fast: float32 [8, 640, 640], P('head'), may hold values from -0.25 to 0.25
- down_fast: float32 [8, 640, 640], P('head'), may hold values from -0.25 to 0.25
- out_gain: float32 [5120], P('head'), may hold values from 0.5 to 1.5
- out_proj: bfloat16 [5120, 5120], P('head'), may hold values from -0.078125 to 0.078125
Outputs:
- mixed: bfloat16 [2, 8192, 5120], P(None, ('ctx', 'head'))
The draws below stay inside these ranges and needn't reach their ends.
All inputs are finite; a program needn't handle non-finite values.
Results may differ from the reference program's by a relative error of at most 0.014.
Values may be sent and summed in bfloat16 or wider, within the bound.
No kernel may reach another device: no remote copies, remote signals or barrier semaphores. Data moves between devices by JAX's collectives and lax.ppermute only.
A program may use at most 128 MiB of HBM per device.

```python
import math
import jax
import jax.numpy as jnp
from jax import lax

HD = 640
BLOCKS = 2
HEADS = 8
D = 5120
BLOCK = 8192


def steps_of(rng, extent, split, low, largest):
    loudness = 1.0
    for position, parts in split:
        heights = jax.random.uniform(jax.random.fold_in(jax.random.fold_in(rng, 6), position), (parts,), jnp.float32, low / len(split), largest / len(split))
        loudness = loudness * jnp.repeat(jnp.exp(heights), extent[position] // parts).reshape((-1,) + (1,) * (len(extent) - 1 - position))
    return loudness


def normal_values(key, shape, deviation, limit, cuts=(), held_as=jnp.bfloat16):
    entries = jax.random.normal(key, shape, jnp.float32) * deviation
    if len(cuts) > 0:
        entries = steps_of(key, shape, cuts, -0.22, 0.18) * entries
    return jnp.clip(entries, min=-limit, max=limit).astype(held_as)


def setup_inputs(seed: int = 0) -> dict:
    key_of = jax.random.split(jax.random.key(seed), 10)
    return {
        "queries": normal_values(key_of[0], (BLOCKS, BLOCK, D), 1.0, 6.0, ((1, 128),)),
        "keys": normal_values(key_of[1], (BLOCKS, BLOCK, D), 1.0, 6.0, ((1, 128),)),
        "values": normal_values(key_of[2], (BLOCKS, BLOCK, D), 1.0, 6.0, ((1, 128),)),
        "rates": jnp.clip(jnp.exp(math.log(0.0013046265) - 2.301124 * jax.random.uniform(key_of[3], (BLOCKS, BLOCK, HEADS), jnp.float32) ** steps_of(key_of[3], (BLOCKS, BLOCK, HEADS), ((1, 128),), -0.2, 0.2)), 0.00013065338, 0.0013046265).astype(jnp.bfloat16),
        "gate_fast": normal_values(key_of[4], (HEADS, HD, HD), HD ** -0.5, 0.25, ((0, 8),), jnp.float32),
        "up_fast": normal_values(key_of[5], (HEADS, HD, HD), HD ** -0.5, 0.25, ((0, 8),), jnp.float32),
        "down_fast": normal_values(key_of[6], (HEADS, HD, HD), HD ** -0.5, 0.25, ((0, 8),), jnp.float32),
        "out_gain": jnp.clip(1.0 + 0.1 * jax.random.normal(key_of[7], (D,), jnp.float32), 0.5, 1.5),
        "out_proj": normal_values(key_of[8], (D, D), D ** -0.5, 0.078125, ((0, 8),)),
    }


highest = lax.Precision.HIGHEST

def matmul(left, right):
    return jnp.dot(left, right, precision=highest, preferred_element_type=jnp.float32)

def contract_rows(left, right):
    return lax.dot_general(left, right, (((0,), (0,)), ((), ())), precision=highest, preferred_element_type=jnp.float32)

def contract_cols(left, right):
    return lax.dot_general(left, right, (((1,), (1,)), ((), ())), precision=highest, preferred_element_type=jnp.float32)

def fast_grads(key_rows, value_rows, rate_rows, w_gate, w_up, w_down):
    pre_gate = matmul(key_rows, w_gate)
    pre_up = matmul(key_rows, w_up)
    sigma = jax.nn.sigmoid(pre_gate)
    silu_gate = pre_gate * sigma
    hidden = silu_gate * pre_up
    target = value_rows * rate_rows[:, None]
    grad_down = contract_rows(hidden, target)
    back = contract_cols(target, w_down)
    grad_gate = contract_rows(key_rows, back * pre_up * sigma * (1.0 + pre_gate * (1.0 - sigma)))
    grad_up = contract_rows(key_rows, back * silu_gate)
    return (grad_gate, grad_up, grad_down)

def renorm(matrix, target_norm):
    return matrix * (target_norm * lax.rsqrt(lax.optimization_barrier(jnp.sum(matrix * matrix, axis=-2)) + 1e-06))[..., None, :]

def fast_apply(query_rows, w_gate, w_up, w_down):
    pre_gate = matmul(query_rows, w_gate)
    hidden = pre_gate * jax.nn.sigmoid(pre_gate) * matmul(query_rows, w_up)
    return matmul(hidden, w_down)

def head_norm(out_rows, gain_rows):
    return out_rows * lax.rsqrt(lax.optimization_barrier(jnp.mean(out_rows * out_rows, axis=-1, keepdims=True)) + 1e-05) * gain_rows

def reference(queries, keys, values, rates, gate_fast, up_fast, down_fast, out_gain, out_proj):
    normed_all = [[] for block_index in range(BLOCKS)]
    for head_index in range(HEADS):
        col_start = head_index * HD
        col_stop = col_start + HD
        weights = (gate_fast[head_index], up_fast[head_index], down_fast[head_index])
        norms = tuple((jnp.sqrt(lax.optimization_barrier(jnp.sum(matrix * matrix, axis=0))) for matrix in weights))
        for block_index in range(BLOCKS):
            key_rows = keys[block_index, :, col_start:col_stop].astype(jnp.float32)
            value_rows = values[block_index, :, col_start:col_stop].astype(jnp.float32)
            query_rows = queries[block_index, :, col_start:col_stop].astype(jnp.float32)
            rate_rows = rates[block_index, :, head_index].astype(jnp.float32)
            grads = fast_grads(key_rows, value_rows, rate_rows, weights[0], weights[1], weights[2])
            weights = tuple((renorm(matrix + grad, norm) for matrix, grad, norm in zip(weights, grads, norms)))
            out_rows = fast_apply(query_rows, weights[0], weights[1], weights[2])
            normed_all[block_index].append(head_norm(out_rows, out_gain[col_start:col_stop]).astype(jnp.bfloat16))
    mixed = []
    for block_index in range(BLOCKS):
        normed = jnp.concatenate(normed_all[block_index], axis=1)
        mixed.append(jnp.dot(normed, out_proj, preferred_element_type=jnp.float32).astype(jnp.bfloat16))
    return jnp.stack(mixed, 0)
```

```python
import jax
import jax.numpy as jnp
from jax import lax
from jax.experimental import pallas as pl
from jax.experimental.pallas import tpu as pltpu
from jax.sharding import Mesh, PartitionSpec as P

F32 = jnp.float32
BF16 = jnp.bfloat16
AXES = ("x", "yh", "core", "z", "yl")
SIZES = (4, 2, 2, 4, 2)
HD = 640
WIDE = 5120
TOK = 64
HALF = 320
PART = 80
PIECE = 240
COLS = 2560
SLAB = 1280
TILE = 640


VMEM = pl.BlockSpec(memory_space=pltpu.VMEM)
SMEM = pl.BlockSpec(memory_space=pltpu.SMEM)


def cost(flops, moved):
    return pl.CostEstimate(flops=flops, bytes_accessed=moved, transcendentals=0)


def room(mib):
    return pltpu.CompilerParams(vmem_limit_bytes=mib << 20)


def nt(left, right):
    return lax.dot_general(left, right, (((1,), (1,)), ((), ())), preferred_element_type=F32)


def tn(left, right):
    return lax.dot_general(left, right, (((0,), (0,)), ((), ())), preferred_element_type=F32)


def nn(left, right):
    return lax.dot_general(left, right, (((1,), (0,)), ((), ())), preferred_element_type=F32)


def shift(array, axis, by, size):
    return lax.ppermute(array, axis, [(i, (i + by) % size) for i in range(size)])


def to_heads(array):
    return lax.all_to_all(array, ("z", "yl"), 0, 0, tiled=True)


def add(*terms):
    total = terms[0].astype(F32)
    for term in terms[1:]:
        total = total + term.astype(F32)
    return total


def split(matrix):
    high = matrix.astype(BF16)
    return high, (matrix - high.astype(F32)).astype(BF16)


def pack_keys(key_block, value_block, rate_block, out_ref):
    rates = rate_block[0].astype(F32)
    for head in range(8):
        cols = slice(head * HD, (head + 1) * HD)
        out_ref[head, :TOK, :] = key_block[0, :, cols]
        target = value_block[0, :, cols].astype(F32) * rates[:, head : head + 1]
        out_ref[head, TOK : 2 * TOK, :] = target.astype(BF16)


def pack_first_kernel(key_ref, value_ref, rate_ref, out_ref):
    pack_keys(key_ref, value_ref, rate_ref, out_ref)


def pack_second_kernel(key_ref, value_ref, rate_ref, query_ref, out_ref):
    pack_keys(key_ref, value_ref, rate_ref, out_ref)
    for head in range(8):
        for block in range(2):
            start = (2 + block) * TOK
            cols = slice(head * HD, (head + 1) * HD)
            out_ref[head, start : start + TOK, :] = query_ref[block, :, cols]


def block_of(block, width):
    return pl.BlockSpec((1, TOK, width), lambda i: (block, 0, 0))


def pack_first(keys, values, rates):
    return pl.pallas_call(
        pack_first_kernel,
        grid=(1,),
        in_specs=[block_of(0, WIDE), block_of(0, WIDE), block_of(0, 8)],
        out_specs=pl.BlockSpec((8, 2 * TOK, HD), lambda i: (0, 0, 0)),
        out_shape=jax.ShapeDtypeStruct((8, 2 * TOK, HD), BF16),
        cost_estimate=cost(1 << 20, 4 * TOK * WIDE * 2),
        name="pack_first",
    )(keys, values, rates)


def pack_second(keys, values, rates, queries):
    return pl.pallas_call(
        pack_second_kernel,
        grid=(1,),
        in_specs=[
            block_of(1, WIDE),
            block_of(1, WIDE),
            block_of(1, 8),
            pl.BlockSpec((2, TOK, WIDE), lambda i: (0, 0, 0)),
        ],
        out_specs=pl.BlockSpec((8, 4 * TOK, HD), lambda i: (0, 0, 0)),
        out_shape=jax.ShapeDtypeStruct((8, 4 * TOK, HD), BF16),
        cost_estimate=cost(1 << 20, 8 * TOK * WIDE * 2),
        name="pack_second",
    )(keys, values, rates, queries)


def start_kernel(gate_ref, up_ref, down_ref, master_ref, high_ref, low_ref, row_norm_ref, col_norm_ref):
    for slot, ref in ((0, gate_ref), (1, up_ref)):
        matrix = ref[0].T
        master_ref[slot] = matrix
        high_ref[slot], low_ref[slot] = split(matrix)
        row_norm_ref[slot] = jnp.sqrt(jnp.sum(matrix * matrix, axis=1, keepdims=True))
    matrix = down_ref[0]
    master_ref[2] = matrix
    high_ref[2], low_ref[2] = split(matrix)
    col_norm_ref[...] = jnp.sqrt(jnp.sum(matrix * matrix, axis=0, keepdims=True))


def start_weights(gate, up, down):
    return pl.pallas_call(
        start_kernel,
        in_specs=[VMEM] * 3,
        out_specs=[VMEM] * 5,
        out_shape=[
            jax.ShapeDtypeStruct((3, HD, HD), F32),
            jax.ShapeDtypeStruct((3, HD, HD), BF16),
            jax.ShapeDtypeStruct((3, HD, HD), BF16),
            jax.ShapeDtypeStruct((2, HD, 1), F32),
            jax.ShapeDtypeStruct((1, HD), F32),
        ],
        cost_estimate=cost(1 << 24, 3 * HD * HD * 10),
        name="start_weights",
    )(gate, up, down)


def renorm_kernel(place_ref, master_ref, row_norm_ref, col_norm_ref, *refs):
    pieces, (new_ref, high_ref, low_ref) = refs[:8], refs[8:]
    core, x = place_ref[0], place_ref[1]
    squares = jnp.zeros((8, HD), F32)
    for index, piece in enumerate(pieces):
        side, d = index // 4, index % 4
        owner = core if side == 0 else 1 - core
        start = pl.multiple_of(owner * HALF + lax.rem(x + 4 - d, 4) * PART, 16)
        for slot in range(2):
            rows = pl.ds(start, PART)
            moved = master_ref[slot, rows, :] + piece[slot * PART : (slot + 1) * PART, :].astype(F32)
            scale = row_norm_ref[slot, rows, :] * lax.rsqrt(
                jnp.sum(moved * moved, axis=1, keepdims=True) + 1e-6
            )
            moved = moved * scale
            new_ref[slot, rows, :] = moved
            high_ref[slot, rows, :], low_ref[slot, rows, :] = split(moved)
        rows = pl.ds(start, PART)
        moved = master_ref[2, rows, :] + piece[2 * PART :, :].astype(F32)
        new_ref[2, rows, :] = moved
        squares = squares + jnp.sum((moved * moved).reshape(PART // 8, 8, HD), axis=0)
    scale = col_norm_ref[...] * lax.rsqrt(jnp.sum(squares, axis=0, keepdims=True) + 1e-6)
    moved = new_ref[2] * scale
    new_ref[2] = moved
    high_ref[2], low_ref[2] = split(moved)


def renorm(place, master, row_norm, col_norm, pieces):
    return pl.pallas_call(
        renorm_kernel,
        in_specs=[SMEM] + [VMEM] * 11,
        out_specs=[VMEM] * 3,
        out_shape=[
            jax.ShapeDtypeStruct((3, HD, HD), F32),
            jax.ShapeDtypeStruct((3, HD, HD), BF16),
            jax.ShapeDtypeStruct((3, HD, HD), BF16),
        ],
        compiler_params=room(24),
        cost_estimate=cost(1 << 24, 3 * HD * HD * 12),
        name="renorm",
    )(place, master, row_norm, col_norm, *pieces)


def grads_kernel(place_ref, high_ref, low_ref, *refs):
    outs = refs[2:6]
    keys, targets, hidden, into_gate, into_up, total = refs[6:]
    core, x = place_ref[0], place_ref[1]
    for side in range(2):
        for index in range(8):
            rows = pl.ds((side * 8 + index) * TOK, TOK)
            keys[rows, :] = refs[side][index, :TOK, :]
            targets[rows, :] = refs[side][index, TOK : 2 * TOK, :]
    half = pl.ds(pl.multiple_of(core * HALF, HALF), HALF)

    def chunk(step, carry):
        rows = pl.ds(pl.multiple_of(step * 256, 256), 256)
        key = keys[rows, :]
        target = targets[rows, :]
        gate = nt(key, high_ref[0, half, :]) + nt(key, low_ref[0, half, :])
        up = nt(key, high_ref[1, half, :]) + nt(key, low_ref[1, half, :])
        back = nt(target, high_ref[2, half, :]) + nt(target, low_ref[2, half, :])
        sigma = jax.nn.sigmoid(gate)
        silu = gate * sigma
        hidden[rows, :] = (silu * up).astype(BF16)
        into_gate[rows, :] = (back * up * sigma * (1.0 + gate * (1.0 - sigma))).astype(BF16)
        into_up[rows, :] = (back * silu).astype(BF16)
        return carry

    lax.fori_loop(0, 4, chunk, 0)
    total[0] = tn(into_gate[...], keys[...])
    total[1] = tn(into_up[...], keys[...])
    total[2] = tn(hidden[...], targets[...])
    for d in range(4):
        rows = pl.ds(pl.multiple_of(lax.rem(x + d, 4) * PART, 16), PART)
        for slot in range(3):
            outs[d][slot * PART : (slot + 1) * PART, :] = total[slot, rows, :].astype(outs[d].dtype)


def grads(place, weights, near, far):
    part = pl.BlockSpec((8, 2 * TOK, HD), lambda i: (0, 0, 0))
    return pl.pallas_call(
        grads_kernel,
        grid=(1,),
        in_specs=[SMEM] + [pl.BlockSpec((3, HD, HD), lambda i: (0, 0, 0))] * 2 + [part] * 2,
        out_specs=[pl.BlockSpec((PIECE, HD), lambda i: (0, 0))] * 4,
        out_shape=[jax.ShapeDtypeStruct((PIECE, HD), F32 if d == 0 else BF16) for d in range(4)],
        scratch_shapes=[
            pltpu.VMEM((16 * TOK, HD), BF16),
            pltpu.VMEM((16 * TOK, HD), BF16),
            pltpu.VMEM((16 * TOK, HALF), BF16),
            pltpu.VMEM((16 * TOK, HALF), BF16),
            pltpu.VMEM((16 * TOK, HALF), BF16),
            pltpu.VMEM((3, HALF, HD), F32),
        ],
        cost_estimate=cost(12 * 16 * TOK * HALF * HD, 8 << 20),
        compiler_params=room(24),
        name="grads",
    )(place, *weights, near, far)


def sum_over_ctx(parts):
    received = {d: shift(parts[d], "x", d, 4) for d in (1, 3, 2)}
    mine = add(parts[0], received[1], received[3], received[2])
    other = shift(mine.astype(BF16), "yh", 1, 2)
    mine = add(mine, other).astype(BF16)
    near = {d: shift(mine, "x", d, 4) for d in (1, 3, 2)}
    pieces = [mine, near[1], near[2], near[3]]
    far = {d: shift(pieces[d], "core", 1, 2) for d in (0, 1, 3, 2)}
    return pieces + [far[d] for d in range(4)]


def apply_kernel(place_ref, high_ref, low_ref, gain_ref, query_ref, *refs):
    outs, rows_all = refs[:4], refs[4]
    z, yl = place_ref[2], place_ref[3]
    for d in range(4):
        for dy in range(2):
            source = lax.rem(z + 4 - d, 4) * 2 + lax.rem(yl + dy, 2)
            rows_all[pl.ds((d * 2 + dy) * TOK, TOK), :] = query_ref[source]
    gain = gain_ref[...]
    for step in range(2):
        query = rows_all[step * 4 * TOK : (step + 1) * 4 * TOK, :]
        gate = nt(query, high_ref[0]) + nt(query, low_ref[0])
        up = nt(query, high_ref[1]) + nt(query, low_ref[1])
        hidden = (gate * jax.nn.sigmoid(gate) * up).astype(BF16)
        out = nn(hidden, high_ref[2])
        mean = jnp.sum(out * out, axis=1, keepdims=True) * (1.0 / HD)
        out = (out * lax.rsqrt(mean + 1e-5) * gain).astype(BF16)
        outs[2 * step][...] = out[: 2 * TOK]
        outs[2 * step + 1][...] = out[2 * TOK :]


def apply_weights(block, place, weights, gain, queries):
    return pl.pallas_call(
        apply_kernel,
        grid=(1,),
        in_specs=[
            SMEM,
            pl.BlockSpec((3, HD, HD), lambda i: (0, 0, 0)),
            pl.BlockSpec((2, HD, HD), lambda i: (0, 0, 0)),
            pl.BlockSpec((1, HD), lambda i: (0, 0)),
            pl.BlockSpec((8, TOK, HD), lambda i: (0, 2 + block, 0)),
        ],
        out_specs=[pl.BlockSpec((2 * TOK, HD), lambda i: (0, 0))] * 4,
        out_shape=[jax.ShapeDtypeStruct((2 * TOK, HD), BF16)] * 4,
        scratch_shapes=[pltpu.VMEM((8 * TOK, HD), BF16)],
        compiler_params=room(24),
        cost_estimate=cost(10 * 8 * TOK * HD * HD, 5 << 20),
        name="apply_weights",
    )(place, *weights, gain, queries)


def project_body(side, part_of_side, place_ref, *refs):
    rows, own, parts = refs[:8], refs[8], refs[9:15]
    keep_ref, send_ref, both, slots, sems = refs[15:]
    step = pl.program_id(0)
    tiles = SLAB // TILE
    base = part_of_side * SLAB
    half = place_ref[0] if side == 0 else 1 - place_ref[0]

    def copies(t):
        slot = lax.rem(t, 2)
        cols = pl.ds(pl.multiple_of(base + t * TILE, TILE), TILE)
        own_cols = pl.ds(pl.multiple_of(half * COLS + base + t * TILE, TILE), TILE)
        pairs = [(own.at[:, own_cols], slots.at[slot, pl.ds(0, HD)])]
        for index, part in enumerate(parts):
            start = HD + index * HALF
            pairs.append((part.at[:, cols], slots.at[slot, pl.ds(start, HALF)]))
        return [
            pltpu.make_async_copy(source, target, sems.at[slot, index])
            for index, (source, target) in enumerate(pairs)
        ]

    @pl.when(step == 0)
    def _():
        for copy in copies(step):
            copy.start()
        for block in range(2):
            for d in range(4):
                piece = rows[block * 4 + d]
                cols = slice(d * HD, (d + 1) * HD)
                both[block * TOK : (block + 1) * TOK, cols] = piece[:TOK, :]
                both[(2 + block) * TOK : (3 + block) * TOK, cols] = piece[TOK:, :]

    @pl.when(step + 1 < tiles)
    def _():
        for copy in copies(step + 1):
            copy.start()

    for copy in copies(step):
        copy.wait()
    total = nn(both[...], slots[lax.rem(step, 2)])
    keep_ref[...] = total[: 2 * TOK].astype(BF16)
    send_ref[...] = total[2 * TOK :].astype(BF16)


def project(side, part_of_side, place, rows, own, parts):
    tiles = SLAB // TILE
    out = pl.BlockSpec((2 * TOK, TILE), lambda t, place_ref: (0, t))
    return pl.pallas_call(
        lambda *refs: project_body(side, part_of_side, *refs),
        grid_spec=pltpu.PrefetchScalarGridSpec(
            num_scalar_prefetch=1,
            grid=(tiles,),
            in_specs=[pl.BlockSpec((2 * TOK, HD), lambda t, place_ref: (0, 0))] * 8
            + [pl.BlockSpec(memory_space=pl.ANY)] * 7,
            out_specs=[out, out],
            scratch_shapes=[
                pltpu.VMEM((4 * TOK, 4 * HD), BF16),
                pltpu.VMEM((2, 4 * HD, TILE), BF16),
                pltpu.SemaphoreType.DMA((2, 7)),
            ],
        ),
        out_shape=[jax.ShapeDtypeStruct((2 * TOK, SLAB), BF16)] * 2,
        compiler_params=room(24),
        cost_estimate=cost(2 * 256 * 2560 * SLAB, 2560 * SLAB * 2),
    )(place, *rows, own, *parts)


def finish_kernel(place_ref, *refs):
    out_ref = refs[-1]
    for index in range(WIDE // SLAB):
        keep, got = refs[index * 2 : index * 2 + 2]
        side, part_of_side = divmod(index, COLS // SLAB)
        half = place_ref[0] if side == 0 else 1 - place_ref[0]
        cols = pl.ds(pl.multiple_of(half * COLS + part_of_side * SLAB, 128), SLAB)
        for block in range(2):
            rows = pl.ds(block * TOK, TOK)
            total = keep[rows, :].astype(F32) + got[rows, :].astype(F32)
            out_ref[block, :, cols] = total.astype(BF16)


def finish(place, parts):
    return pl.pallas_call(
        finish_kernel,
        in_specs=[SMEM] + [VMEM] * 8,
        out_specs=VMEM,
        out_shape=jax.ShapeDtypeStruct((2, TOK, WIDE), BF16),
        compiler_params=room(24),
        cost_estimate=cost(1 << 20, 6 << 20),
        name="finish",
    )(place, *parts)


def per_device(queries, keys, values, rates, gate_fast, up_fast, down_fast, out_gain, out_proj):
    core = lax.axis_index("core")
    place = jnp.stack([core] + [lax.axis_index(name) for name in ("x", "z", "yl")])
    place = place.astype(jnp.int32)
    gain = out_gain.reshape(1, HD)

    first = to_heads(pack_first(keys, values, rates))
    first_far = shift(first, "core", 1, 2)
    second = to_heads(pack_second(keys, values, rates, queries))
    second_far = shift(second, "core", 1, 2)

    low = lax.dynamic_slice(out_proj, (0, core * COLS), (HALF, COLS))
    high = lax.dynamic_slice(out_proj, (HALF, core * COLS), (HALF, COLS))
    before_low = shift(low, "z", 1, 4)
    after_high = shift(high, "z", 3, 4)
    before_high = shift(high, "z", 1, 4)
    after_low = shift(low, "z", 3, 4)
    far_low = shift(before_low, "z", 1, 4)
    far_high = shift(after_high, "z", 3, 4)
    own_side = (before_low, before_high, far_low, far_high, after_low, after_high)
    other_near = [shift(own_side[i], "core", 1, 2) for i in (0, 1, 4, 5)]
    other_far = [shift(part, "core", 1, 2) for part in (far_low, far_high)]
    other_side = (*other_near[:2], *other_far, *other_near[2:])

    master, *weights, row_norm, col_norm = start_weights(gate_fast, up_fast, down_fast)

    def spread(block, weights):
        rows = apply_weights(block, place, weights, gain, second)
        back = {d: shift(rows[d], "z", 4 - d, 4) for d in (2, 1, 3)}
        return [rows[0], back[3], back[2], back[1]]

    total = sum_over_ctx(grads(place, weights, first, first_far))
    master, *weights = renorm(place, master, row_norm, col_norm, total)
    parts = grads(place, weights, second, second_far)
    total = sum_over_ctx(parts)
    rows = spread(0, weights)
    master, *weights = renorm(place, master, row_norm, col_norm, total)
    rows += spread(1, weights)
    mixed = []
    for side, gathered in enumerate((own_side, other_side)):
        for part_of_side in range(COLS // SLAB):
            keep, send = project(side, part_of_side, place, rows, out_proj, gathered)
            mixed += [keep, shift(send, "yl", 1, 2)]
    return finish(place, mixed)


def solution(mesh):
    fine = Mesh(mesh.devices.reshape(SIZES), AXES)
    tokens = P(None, AXES, None)
    head = ("z", "yl")
    placed = (
        tokens,
        tokens,
        tokens,
        tokens,
        P(head, None, None),
        P(head, None, None),
        P(head, None, None),
        P(head),
        P(head, None),
    )
    return jax.shard_map(per_device, mesh=fine, in_specs=placed, out_specs=tokens, check_vma=False)
```

```python
import jax
import jax.numpy as jnp
from jax import lax
from jax.experimental import pallas as pl
from jax.experimental.pallas import tpu as pltpu
from jax.sharding import Mesh, PartitionSpec as P

F32 = jnp.float32
BF16 = jnp.bfloat16
AXES = ("x", "yh", "core", "z", "yl")
SIZES = (4, 2, 2, 4, 2)
HD = 640
WIDE = 5120
TOK = 64
HALF = 320
PART = 80
PIECE = 240
COLS = 2560
SLAB = 1280
TILE = 640


VMEM = pl.BlockSpec(memory_space=pltpu.VMEM)
SMEM = pl.BlockSpec(memory_space=pltpu.SMEM)


def cost(flops, moved):
    return pl.CostEstimate(flops=flops, bytes_accessed=moved, transcendentals=0)


def room(mib):
    return pltpu.CompilerParams(vmem_limit_bytes=mib << 20)


def nt(left, right):
    return lax.dot_general(left, right, (((1,), (1,)), ((), ())), preferred_element_type=F32)


def nn(left, right):
    return lax.dot_general(left, right, (((1,), (0,)), ((), ())), preferred_element_type=F32)


def shift(array, axis, by, size):
    return lax.ppermute(array, axis, [(i, (i + by) % size) for i in range(size)])


def to_heads(array):
    return lax.all_to_all(array, ("z", "yl"), 0, 0, tiled=True)


def add(*terms):
    total = terms[0].astype(F32)
    for term in terms[1:]:
        total = total + term.astype(F32)
    return total


def split(matrix):
    high = matrix.astype(BF16)
    return high, (matrix - high.astype(F32)).astype(BF16)


def pack_keys(key_block, value_block, rate_block, out_ref):
    rates = rate_block[0].astype(F32)
    row = lax.broadcasted_iota(jnp.int32, (TOK, TOK), 0)
    lane = lax.broadcasted_iota(jnp.int32, (TOK, TOK), 1)
    for head in range(8):
        cols = slice(head * HD, (head + 1) * HD)
        out_ref[head, :TOK, :] = key_block[0, :, cols]
        spread = jnp.broadcast_to(rates[head : head + 1, :], (TOK, TOK))
        rate = jnp.sum(jnp.where(row == lane, spread, 0.0), axis=1, keepdims=True)
        target = value_block[0, :, cols].astype(F32) * rate
        out_ref[head, TOK : 2 * TOK, :] = target.astype(BF16)


def pack_first_kernel(key_ref, value_ref, rate_ref, out_ref):
    pack_keys(key_ref, value_ref, rate_ref, out_ref)


def pack_second_kernel(key_ref, value_ref, rate_ref, query_ref, out_ref):
    pack_keys(key_ref, value_ref, rate_ref, out_ref)
    for head in range(8):
        for block in range(2):
            start = (2 + block) * TOK
            cols = slice(head * HD, (head + 1) * HD)
            out_ref[head, start : start + TOK, :] = query_ref[block, :, cols]


def block_of(block, width):
    return pl.BlockSpec((1, TOK, width), lambda i: (block, 0, 0))


def rates_of(block):
    return pl.BlockSpec((1, 8, TOK), lambda i: (block, 0, 0))


def pack_first(keys, values, rates):
    return pl.pallas_call(
        pack_first_kernel,
        grid=(1,),
        in_specs=[block_of(0, WIDE), block_of(0, WIDE), rates_of(0)],
        out_specs=pl.BlockSpec((8, 2 * TOK, HD), lambda i: (0, 0, 0)),
        out_shape=jax.ShapeDtypeStruct((8, 2 * TOK, HD), BF16),
        cost_estimate=cost(1 << 20, 4 * TOK * WIDE * 2),
        name="pack_first",
    )(keys, values, rates)


def pack_second(keys, values, rates, queries):
    return pl.pallas_call(
        pack_second_kernel,
        grid=(1,),
        in_specs=[
            block_of(1, WIDE),
            block_of(1, WIDE),
            rates_of(1),
            pl.BlockSpec((2, TOK, WIDE), lambda i: (0, 0, 0)),
        ],
        out_specs=pl.BlockSpec((8, 4 * TOK, HD), lambda i: (0, 0, 0)),
        out_shape=jax.ShapeDtypeStruct((8, 4 * TOK, HD), BF16),
        cost_estimate=cost(1 << 20, 8 * TOK * WIDE * 2),
        name="pack_second",
    )(keys, values, rates, queries)


def start_half_kernel(place_ref, gate_ref, up_ref, down_ref, high_ref, low_ref, turned):
    half = pl.ds(pl.multiple_of(place_ref[0] * HALF, HALF), HALF)
    for slot, ref in ((0, gate_ref), (1, up_ref)):
        turned[...] = ref[0].T
        high_ref[slot], low_ref[slot] = split(turned[half, :])
    high_ref[2], low_ref[2] = split(down_ref[0, half, :])


def start_half(place, gate, up, down):
    return pl.pallas_call(
        start_half_kernel,
        in_specs=[SMEM] + [VMEM] * 3,
        out_specs=[VMEM] * 2,
        out_shape=[pltpu.VMEM((3, HALF, HD), BF16)] * 2,
        scratch_shapes=[pltpu.VMEM((HD, HD), F32)],
        compiler_params=room(16),
        cost_estimate=cost(1 << 24, 3 * HD * HD * 6),
        name="start_half",
    )(place, gate, up, down)


def start_full_kernel(gate_ref, up_ref, down_ref, master_ref, row_norm_ref, col_norm_ref):
    for slot, ref in ((0, gate_ref), (1, up_ref)):
        matrix = ref[0].T
        master_ref[slot] = matrix
        row_norm_ref[slot] = jnp.sqrt(jnp.sum(matrix * matrix, axis=1, keepdims=True))
    matrix = down_ref[0]
    master_ref[2] = matrix
    col_norm_ref[...] = jnp.sqrt(jnp.sum(matrix * matrix, axis=0, keepdims=True))


def start_full(gate, up, down):
    return pl.pallas_call(
        start_full_kernel,
        in_specs=[VMEM] * 3,
        out_specs=[VMEM] * 3,
        out_shape=[
            pltpu.VMEM((3, HD, HD), F32),
            pltpu.VMEM((2, HD, 1), F32),
            pltpu.VMEM((1, HD), F32),
        ],
        compiler_params=room(16),
        cost_estimate=cost(1 << 24, 3 * HD * HD * 8),
        name="start_full",
    )(gate, up, down)


def renorm_kernel(count, place_ref, *refs):
    old_refs, (row_norm_ref, col_norm_ref) = refs[:count], refs[count : count + 2]
    pieces, (high_ref, low_ref, down_ref) = refs[count + 2 : count + 10], refs[count + 10 :]
    core, x = place_ref[0], place_ref[1]
    squares = jnp.zeros((8, HD), F32)

    def moved_rows(slot, rows, step):
        total = step.astype(F32)
        for old_ref in old_refs:
            total = total + old_ref[slot, rows, :].astype(F32)
        return total

    for index, piece in enumerate(pieces):
        side, d = index // 4, index % 4
        owner = core if side == 0 else 1 - core
        start = pl.multiple_of(owner * HALF + lax.rem(x + 4 - d, 4) * PART, 16)
        rows = pl.ds(start, PART)
        for slot in range(2):
            moved = moved_rows(slot, rows, piece[slot * PART : (slot + 1) * PART, :])
            scale = row_norm_ref[slot, rows, :] * lax.rsqrt(
                jnp.sum(moved * moved, axis=1, keepdims=True) + 1e-6
            )
            high_ref[slot, rows, :], low_ref[slot, rows, :] = split(moved * scale)
        moved = moved_rows(2, rows, piece[2 * PART :, :])
        down_ref[rows, :] = moved
        squares = squares + jnp.sum((moved * moved).reshape(PART // 8, 8, HD), axis=0)
    scale = col_norm_ref[...] * lax.rsqrt(jnp.sum(squares, axis=0, keepdims=True) + 1e-6)
    high_ref[2], low_ref[2] = split(down_ref[...] * scale)


def renorm(place, weights, row_norm, col_norm, pieces):
    return pl.pallas_call(
        lambda *refs: renorm_kernel(len(weights), *refs),
        in_specs=[SMEM] + [VMEM] * (10 + len(weights)),
        out_specs=[VMEM] * 2,
        out_shape=[pltpu.VMEM((3, HD, HD), BF16)] * 2,
        scratch_shapes=[pltpu.VMEM((HD, HD), F32)],
        compiler_params=room(16),
        cost_estimate=cost(1 << 24, 3 * HD * HD * 10),
        name="renorm",
    )(place, *weights, row_norm, col_norm, *pieces)


def grads_kernel(place_ref, high_ref, low_ref, near_ref, far_ref, *refs):
    outs, (tokens, inner, total) = refs[:4], refs[4:]
    core, x = place_ref[0], place_ref[1]
    for side, ref in enumerate((near_ref, far_ref)):
        for index in range(8):
            rows = pl.ds((side * 8 + index) * TOK, TOK)
            tokens[0, rows, :] = ref[index, :TOK, :]
            tokens[1, rows, :] = ref[index, TOK : 2 * TOK, :]
    height = high_ref.shape[1]
    half = pl.ds(pl.multiple_of(core * (height - HALF), HALF), HALF)

    def product(slot, rows):
        return nt(high_ref[slot, half, :], rows) + nt(low_ref[slot, half, :], rows)

    def chunk(step, carry):
        rows = pl.ds(pl.multiple_of(step * 256, 256), 256)
        key = tokens[0, rows, :]
        gate = product(0, key)
        up = product(1, key)
        back = product(2, tokens[1, rows, :])
        sigma = jax.nn.sigmoid(gate)
        silu = gate * sigma
        inner[0, :, rows] = (back * up * sigma * (1.0 + gate * (1.0 - sigma))).astype(BF16)
        inner[1, :, rows] = (back * silu).astype(BF16)
        inner[2, :, rows] = (silu * up).astype(BF16)
        return carry

    lax.fori_loop(0, 4, chunk, 0)

    def finish(slot, carry):
        total[slot] = nn(inner[slot], tokens[slot // 2])
        return carry

    lax.fori_loop(0, 3, finish, 0)
    for d in range(4):
        rows = pl.ds(pl.multiple_of(lax.rem(x + d, 4) * PART, 16), PART)
        for slot in range(3):
            outs[d][slot * PART : (slot + 1) * PART, :] = total[slot, rows, :].astype(outs[d].dtype)


def grads(place, weights, near, far):
    part = pl.BlockSpec((8, 2 * TOK, HD), lambda i: (0, 0, 0))
    held = pl.BlockSpec(weights[0].shape, lambda i: (0, 0, 0))
    return pl.pallas_call(
        grads_kernel,
        grid=(1,),
        in_specs=[SMEM] + [held] * 2 + [part] * 2,
        out_specs=[pl.BlockSpec((PIECE, HD), lambda i: (0, 0))] * 4,
        out_shape=[pltpu.VMEM((PIECE, HD), F32 if d == 0 else BF16) for d in range(4)],
        scratch_shapes=[
            pltpu.VMEM((2, 16 * TOK, HD), BF16),
            pltpu.VMEM((3, HALF, 16 * TOK), BF16),
            pltpu.VMEM((3, HALF, HD), F32),
        ],
        cost_estimate=cost(12 * 16 * TOK * HALF * HD, 8 << 20),
        compiler_params=room(16),
        name="grads",
    )(place, *weights, near, far)


def sum_over_ctx(parts):
    received = {d: shift(parts[d], "x", d, 4) for d in (1, 3, 2)}
    mine = lax.optimization_barrier(add(parts[0], received[1], received[3], received[2]))
    other = shift(mine.astype(BF16), "yh", 1, 2)
    mine = add(mine, other).astype(BF16)
    near = {d: shift(mine, "x", d, 4) for d in (1, 3, 2)}
    pieces = [mine, near[1], near[2], near[3]]
    far = {d: shift(pieces[d], "core", 1, 2) for d in (0, 1, 3, 2)}
    return pieces + [far[d] for d in range(4)]


def apply_kernel(place_ref, high_ref, low_ref, gain_ref, query_ref, *refs):
    outs, (rows_in, rows_out) = refs[:4], refs[4:]
    z, yl = place_ref[2], place_ref[3]
    for d in range(4):
        for dy in range(2):
            source = lax.rem(z + 4 - d, 4) * 2 + lax.rem(yl + dy, 2)
            rows_in[pl.ds((d * 2 + dy) * TOK, TOK), :] = query_ref[source]
    gain = gain_ref[...]

    def chunk(step, carry):
        rows = pl.ds(pl.multiple_of(step * 4 * TOK, 4 * TOK), 4 * TOK)
        query = rows_in[rows, :]
        gate = nt(query, high_ref[0]) + nt(query, low_ref[0])
        up = nt(query, high_ref[1]) + nt(query, low_ref[1])
        hidden = (gate * jax.nn.sigmoid(gate) * up).astype(BF16)
        out = nn(hidden, high_ref[2])
        mean = jnp.sum(out * out, axis=1, keepdims=True) * (1.0 / HD)
        rows_out[rows, :] = (out * lax.rsqrt(mean + 1e-5) * gain).astype(BF16)
        return carry

    lax.fori_loop(0, 2, chunk, 0)
    for d in range(4):
        outs[d][...] = rows_out[d * 2 * TOK : (d + 1) * 2 * TOK, :]


def apply_weights(block, place, weights, gain, queries):
    return pl.pallas_call(
        apply_kernel,
        grid=(1,),
        in_specs=[
            SMEM,
            pl.BlockSpec((3, HD, HD), lambda i: (0, 0, 0)),
            pl.BlockSpec((2, HD, HD), lambda i: (0, 0, 0)),
            pl.BlockSpec((1, HD), lambda i: (0, 0)),
            pl.BlockSpec((8, TOK, HD), lambda i: (0, 2 + block, 0)),
        ],
        out_specs=[pl.BlockSpec((2 * TOK, HD), lambda i: (0, 0))] * 4,
        out_shape=[jax.ShapeDtypeStruct((2 * TOK, HD), BF16)] * 4,
        scratch_shapes=[pltpu.VMEM((8 * TOK, HD), BF16)] * 2,
        compiler_params=room(16),
        cost_estimate=cost(10 * 8 * TOK * HD * HD, 5 << 20),
        name="apply_weights",
    )(place, *weights, gain, queries)


def project_body(side, part_of_side, place_ref, *refs):
    rows, own, parts = refs[:8], refs[8], refs[9:15]
    keep_ref, send_ref, both, slots, total, sems = refs[15:]
    step = pl.program_id(0)
    tiles = SLAB // TILE
    base = part_of_side * SLAB
    half = place_ref[0] if side == 0 else 1 - place_ref[0]

    def copies(t):
        slot = lax.rem(t, 2)
        cols = pl.ds(pl.multiple_of(base + t * TILE, TILE), TILE)
        own_cols = pl.ds(pl.multiple_of(half * COLS + base + t * TILE, TILE), TILE)
        pairs = [(own.at[:, own_cols], slots.at[slot, pl.ds(0, HD)])]
        for index, part in enumerate(parts):
            start = HD + index * HALF
            pairs.append((part.at[:, cols], slots.at[slot, pl.ds(start, HALF)]))
        return [
            pltpu.make_async_copy(source, target, sems.at[slot, index])
            for index, (source, target) in enumerate(pairs)
        ]

    @pl.when(step == 0)
    def _():
        for copy in copies(step):
            copy.start()
        for block in range(2):
            for d in range(4):
                piece = rows[block * 4 + d]
                cols = slice(d * HD, (d + 1) * HD)
                both[block * TOK : (block + 1) * TOK, cols] = piece[:TOK, :]
                both[(2 + block) * TOK : (3 + block) * TOK, cols] = piece[TOK:, :]

    @pl.when(step + 1 < tiles)
    def _():
        for copy in copies(step + 1):
            copy.start()

    for copy in copies(step):
        copy.wait()
    slot = lax.rem(step, 2)

    def depth(k, carry):
        cols = pl.ds(pl.multiple_of(k * 512, 512), 512)
        total[...] += nn(both[:, cols], slots[slot, cols, :])
        return carry

    total[...] = jnp.zeros_like(total)
    lax.fori_loop(0, 5, depth, 0)
    keep_ref[...] = total[: 2 * TOK, :].astype(BF16)
    send_ref[...] = total[2 * TOK :, :].astype(BF16)


def project(side, part_of_side, place, rows, own, parts):
    tiles = SLAB // TILE
    out = pl.BlockSpec((2 * TOK, TILE), lambda t, place_ref: (0, t))
    return pl.pallas_call(
        lambda *refs: project_body(side, part_of_side, *refs),
        grid_spec=pltpu.PrefetchScalarGridSpec(
            num_scalar_prefetch=1,
            grid=(tiles,),
            in_specs=[pl.BlockSpec((2 * TOK, HD), lambda t, place_ref: (0, 0))] * 8
            + [pl.BlockSpec(memory_space=pl.ANY)] * 7,
            out_specs=[out, out],
            scratch_shapes=[
                pltpu.VMEM((4 * TOK, 4 * HD), BF16),
                pltpu.VMEM((2, 4 * HD, TILE), BF16),
                pltpu.VMEM((4 * TOK, TILE), F32),
                pltpu.SemaphoreType.DMA((2, 7)),
            ],
        ),
        out_shape=[jax.ShapeDtypeStruct((2 * TOK, SLAB), BF16)] * 2,
        compiler_params=room(16),
        cost_estimate=cost(2 * 256 * 2560 * SLAB, 2560 * SLAB * 2),
    )(place, *rows, own, *parts)


def finish_kernel(place_ref, *refs):
    out_ref = refs[-1]
    for index in range(WIDE // SLAB):
        keep, got = refs[index * 2 : index * 2 + 2]
        side, part_of_side = divmod(index, COLS // SLAB)
        half = place_ref[0] if side == 0 else 1 - place_ref[0]
        cols = pl.ds(pl.multiple_of(half * COLS + part_of_side * SLAB, 128), SLAB)
        for block in range(2):
            rows = pl.ds(block * TOK, TOK)
            total = keep[rows, :].astype(F32) + got[rows, :].astype(F32)
            out_ref[block, :, cols] = total.astype(BF16)


def finish(place, parts):
    return pl.pallas_call(
        finish_kernel,
        in_specs=[SMEM] + [VMEM] * 8,
        out_specs=VMEM,
        out_shape=jax.ShapeDtypeStruct((2, TOK, WIDE), BF16),
        compiler_params=room(16),
        cost_estimate=cost(1 << 20, 6 << 20),
        name="finish",
    )(place, *parts)


def per_device(queries, keys, values, rates, gate_fast, up_fast, down_fast, out_gain, out_proj):
    core = lax.axis_index("core")
    place = jnp.stack([core] + [lax.axis_index(name) for name in ("x", "z", "yl")])
    place = place.astype(jnp.int32)
    gain = out_gain.reshape(1, HD)
    rates = rates.transpose(0, 2, 1)

    first = to_heads(pack_first(keys, values, rates))
    first_far = shift(first, "core", 1, 2)
    second = to_heads(pack_second(keys, values, rates, queries))
    second_far = shift(second, "core", 1, 2)

    low = lax.dynamic_slice(out_proj, (0, core * COLS), (HALF, COLS))
    high = lax.dynamic_slice(out_proj, (HALF, core * COLS), (HALF, COLS))
    before_low = shift(low, "z", 1, 4)
    after_high = shift(high, "z", 3, 4)
    before_high = shift(high, "z", 1, 4)
    after_low = shift(low, "z", 3, 4)
    far_low = shift(before_low, "z", 1, 4)
    far_high = shift(after_high, "z", 3, 4)
    own_side = (before_low, before_high, far_low, far_high, after_low, after_high)
    other_near = [shift(own_side[i], "core", 1, 2) for i in (0, 1, 4, 5)]
    other_far = [shift(part, "core", 1, 2) for part in (far_low, far_high)]
    other_side = (*other_near[:2], *other_far, *other_near[2:])

    halves = start_half(place, gate_fast, up_fast, down_fast)
    master, row_norm, col_norm = start_full(gate_fast, up_fast, down_fast)

    def spread(block, weights):
        rows = apply_weights(block, place, weights, gain, second)
        back = {d: shift(rows[d], "z", 4 - d, 4) for d in (2, 1, 3)}
        return [rows[0], back[3], back[2], back[1]]

    total = sum_over_ctx(grads(place, halves, first, first_far))
    weights = renorm(place, [master], row_norm, col_norm, total)
    parts = grads(place, weights, second, second_far)
    total = sum_over_ctx(parts)
    rows = spread(0, weights)
    weights = renorm(place, weights, row_norm, col_norm, total)
    rows += spread(1, weights)
    mixed = []
    for side, gathered in enumerate((own_side, other_side)):
        for part_of_side in range(COLS // SLAB):
            keep, send = project(side, part_of_side, place, rows, out_proj, gathered)
            mixed += [keep, shift(send, "yl", 1, 2)]
    return finish(place, mixed)


def solution(mesh):
    fine = Mesh(mesh.devices.reshape(SIZES), AXES)
    tokens = P(None, AXES, None)
    head = ("z", "yl")
    placed = (
        tokens,
        tokens,
        tokens,
        tokens,
        P(head, None, None),
        P(head, None, None),
        P(head, None, None),
        P(head),
        P(head, None),
    )
    return jax.shard_map(per_device, mesh=fine, in_specs=placed, out_specs=tokens, check_vma=False)
```

```python
import jax
import jax.numpy as jnp
from jax import lax
from jax.experimental import pallas as pl
from jax.experimental.pallas import tpu as pltpu
from jax.sharding import Mesh, PartitionSpec as P

F32 = jnp.float32
BF16 = jnp.bfloat16
AXES = ("x", "yh", "core", "z", "yl")
SIZES = (4, 2, 2, 4, 2)
HD = 640
WIDE = 5120
TOK = 64
HALF = 320
PART = 80
PIECE = 240
COLS = 2560
LONG = 1536
WIDTH = 1024
TILE = 512


VMEM = pl.BlockSpec(memory_space=pltpu.VMEM)
SMEM = pl.BlockSpec(memory_space=pltpu.SMEM)


def cost(flops, moved):
    return pl.CostEstimate(flops=flops, bytes_accessed=moved, transcendentals=0)


def room(mib):
    return pltpu.CompilerParams(vmem_limit_bytes=mib << 20)


def nt(left, right):
    return lax.dot_general(left, right, (((1,), (1,)), ((), ())), preferred_element_type=F32)


def nn(left, right):
    return lax.dot_general(left, right, (((1,), (0,)), ((), ())), preferred_element_type=F32)


def shift(array, axis, by, size):
    return lax.ppermute(array, axis, [(i, (i + by) % size) for i in range(size)])


def to_heads(array):
    return lax.all_to_all(array, ("z", "yl"), 0, 0, tiled=True)


def add(*terms):
    total = terms[0].astype(F32)
    for term in terms[1:]:
        total = total + term.astype(F32)
    return total


def split(matrix):
    high = matrix.astype(BF16)
    return high, (matrix - high.astype(F32)).astype(BF16)


def pack_keys(key_block, value_block, rate_block, out_ref):
    rates = rate_block[0].astype(F32)
    row = lax.broadcasted_iota(jnp.int32, (TOK, TOK), 0)
    lane = lax.broadcasted_iota(jnp.int32, (TOK, TOK), 1)
    for head in range(8):
        cols = slice(head * HD, (head + 1) * HD)
        out_ref[head, :TOK, :] = key_block[0, :, cols]
        spread = jnp.broadcast_to(rates[head : head + 1, :], (TOK, TOK))
        rate = jnp.sum(jnp.where(row == lane, spread, 0.0), axis=1, keepdims=True)
        target = value_block[0, :, cols].astype(F32) * rate
        out_ref[head, TOK : 2 * TOK, :] = target.astype(BF16)


def pack_first_kernel(key_ref, value_ref, rate_ref, out_ref):
    pack_keys(key_ref, value_ref, rate_ref, out_ref)


def pack_second_kernel(key_ref, value_ref, rate_ref, query_ref, out_ref):
    pack_keys(key_ref, value_ref, rate_ref, out_ref)
    for head in range(8):
        for block in range(2):
            start = (2 + block) * TOK
            cols = slice(head * HD, (head + 1) * HD)
            out_ref[head, start : start + TOK, :] = query_ref[block, :, cols]


def block_of(block, width):
    return pl.BlockSpec((1, TOK, width), lambda i: (block, 0, 0))


def rates_of(block):
    return pl.BlockSpec((1, 8, TOK), lambda i: (block, 0, 0))


def pack_first(keys, values, rates):
    return pl.pallas_call(
        pack_first_kernel,
        grid=(1,),
        in_specs=[block_of(0, WIDE), block_of(0, WIDE), rates_of(0)],
        out_specs=pl.BlockSpec((8, 2 * TOK, HD), lambda i: (0, 0, 0)),
        out_shape=jax.ShapeDtypeStruct((8, 2 * TOK, HD), BF16),
        cost_estimate=cost(1 << 20, 4 * TOK * WIDE * 2),
        name="pack_first",
    )(keys, values, rates)


def pack_second(keys, values, rates, queries):
    return pl.pallas_call(
        pack_second_kernel,
        grid=(1,),
        in_specs=[
            block_of(1, WIDE),
            block_of(1, WIDE),
            rates_of(1),
            pl.BlockSpec((2, TOK, WIDE), lambda i: (0, 0, 0)),
        ],
        out_specs=pl.BlockSpec((8, 4 * TOK, HD), lambda i: (0, 0, 0)),
        out_shape=jax.ShapeDtypeStruct((8, 4 * TOK, HD), BF16),
        cost_estimate=cost(1 << 20, 8 * TOK * WIDE * 2),
        name="pack_second",
    )(keys, values, rates, queries)


def start_half_kernel(place_ref, gate_ref, up_ref, down_ref, high_ref, low_ref, turned):
    core = place_ref[0]
    half = pl.ds(pl.multiple_of(core * HALF, HALF), HALF)
    tiles = pl.ds(pl.multiple_of(core * 256, 256), 384)
    inside = pl.ds(pl.multiple_of(core * (HALF - 256), 64), HALF)
    for slot, ref in ((0, gate_ref), (1, up_ref)):
        turned[...] = ref[0, :, tiles].T
        high_ref[slot], low_ref[slot] = split(turned[inside, :])
    high_ref[2], low_ref[2] = split(down_ref[0, half, :])


def start_half(place, gate, up, down):
    return pl.pallas_call(
        start_half_kernel,
        in_specs=[SMEM] + [VMEM] * 3,
        out_specs=[VMEM] * 2,
        out_shape=[pltpu.VMEM((3, HALF, HD), BF16)] * 2,
        scratch_shapes=[pltpu.VMEM((384, HD), F32)],
        compiler_params=room(16),
        cost_estimate=cost(1 << 24, 3 * HD * HD * 6),
        name="start_half",
    )(place, gate, up, down)


def start_full_kernel(gate_ref, up_ref, down_ref, master_ref, row_norm_ref, col_norm_ref):
    for slot, ref in ((0, gate_ref), (1, up_ref)):
        matrix = ref[0].T
        master_ref[slot] = matrix
        row_norm_ref[slot] = jnp.sqrt(jnp.sum(matrix * matrix, axis=1, keepdims=True))
    matrix = down_ref[0]
    master_ref[2] = matrix
    col_norm_ref[...] = jnp.sqrt(jnp.sum(matrix * matrix, axis=0, keepdims=True))


def start_full(gate, up, down):
    return pl.pallas_call(
        start_full_kernel,
        in_specs=[VMEM] * 3,
        out_specs=[VMEM] * 3,
        out_shape=[
            pltpu.VMEM((3, HD, HD), F32),
            pltpu.VMEM((2, HD, 1), F32),
            pltpu.VMEM((1, HD), F32),
        ],
        compiler_params=room(16),
        cost_estimate=cost(1 << 24, 3 * HD * HD * 8),
        name="start_full",
    )(gate, up, down)


def renorm_kernel(count, place_ref, *refs):
    old_refs, (row_norm_ref, col_norm_ref) = refs[:count], refs[count : count + 2]
    pieces, (high_ref, low_ref, down_ref) = refs[count + 2 : count + 10], refs[count + 10 :]
    core, x = place_ref[0], place_ref[1]
    squares = jnp.zeros((8, HD), F32)

    def moved_rows(slot, rows, step):
        total = step.astype(F32)
        for old_ref in old_refs:
            total = total + old_ref[slot, rows, :].astype(F32)
        return total

    for index, piece in enumerate(pieces):
        side, d = index // 4, index % 4
        owner = core if side == 0 else 1 - core
        start = pl.multiple_of(owner * HALF + lax.rem(x + 4 - d, 4) * PART, 16)
        rows = pl.ds(start, PART)
        for slot in range(2):
            moved = moved_rows(slot, rows, piece[slot * PART : (slot + 1) * PART, :])
            scale = row_norm_ref[slot, rows, :] * lax.rsqrt(
                jnp.sum(moved * moved, axis=1, keepdims=True) + 1e-6
            )
            high_ref[slot, rows, :], low_ref[slot, rows, :] = split(moved * scale)
        moved = moved_rows(2, rows, piece[2 * PART :, :])
        down_ref[rows, :] = moved
        squares = squares + jnp.sum((moved * moved).reshape(PART // 8, 8, HD), axis=0)
    scale = col_norm_ref[...] * lax.rsqrt(jnp.sum(squares, axis=0, keepdims=True) + 1e-6)
    high_ref[2], low_ref[2] = split(down_ref[...] * scale)


def renorm(place, weights, row_norm, col_norm, pieces):
    return pl.pallas_call(
        lambda *refs: renorm_kernel(len(weights), *refs),
        in_specs=[SMEM] + [VMEM] * (10 + len(weights)),
        out_specs=[VMEM] * 2,
        out_shape=[pltpu.VMEM((3, HD, HD), BF16)] * 2,
        scratch_shapes=[pltpu.VMEM((HD, HD), F32)],
        compiler_params=room(16),
        cost_estimate=cost(1 << 24, 3 * HD * HD * 10),
        name="renorm",
    )(place, *weights, row_norm, col_norm, *pieces)


def grads_kernel(place_ref, high_ref, low_ref, near_ref, far_ref, *refs):
    outs, (tokens, inner, total) = refs[:4], refs[4:]
    core, x = place_ref[0], place_ref[1]
    for side, ref in enumerate((near_ref, far_ref)):
        for index in range(8):
            rows = pl.ds((side * 8 + index) * TOK, TOK)
            tokens[0, rows, :] = ref[index, :TOK, :]
            tokens[1, rows, :] = ref[index, TOK : 2 * TOK, :]
    height = high_ref.shape[1]
    half = pl.ds(pl.multiple_of(core * (height - HALF), HALF), HALF)

    def product(slot, rows):
        return nt(high_ref[slot, half, :], rows) + nt(low_ref[slot, half, :], rows)

    def chunk(step, carry):
        rows = pl.ds(pl.multiple_of(step * 256, 256), 256)
        key = tokens[0, rows, :]
        gate = product(0, key)
        up = product(1, key)
        back = product(2, tokens[1, rows, :])
        sigma = jax.nn.sigmoid(gate)
        silu = gate * sigma
        inner[0, :, rows] = (back * up * sigma * (1.0 + gate * (1.0 - sigma))).astype(BF16)
        inner[1, :, rows] = (back * silu).astype(BF16)
        inner[2, :, rows] = (silu * up).astype(BF16)
        return carry

    lax.fori_loop(0, 4, chunk, 0)

    def finish(slot, carry):
        total[slot] = nn(inner[slot], tokens[slot // 2])
        return carry

    lax.fori_loop(0, 3, finish, 0)
    for d in range(4):
        rows = pl.ds(pl.multiple_of(lax.rem(x + d, 4) * PART, 16), PART)
        for slot in range(3):
            outs[d][slot * PART : (slot + 1) * PART, :] = total[slot, rows, :].astype(outs[d].dtype)


def grads(place, weights, near, far):
    part = pl.BlockSpec((8, 2 * TOK, HD), lambda i: (0, 0, 0))
    held = pl.BlockSpec(weights[0].shape, lambda i: (0, 0, 0))
    return pl.pallas_call(
        grads_kernel,
        grid=(1,),
        in_specs=[SMEM] + [held] * 2 + [part] * 2,
        out_specs=[pl.BlockSpec((PIECE, HD), lambda i: (0, 0))] * 4,
        out_shape=[pltpu.VMEM((PIECE, HD), F32 if d == 0 else BF16) for d in range(4)],
        scratch_shapes=[
            pltpu.VMEM((2, 16 * TOK, HD), BF16),
            pltpu.VMEM((3, HALF, 16 * TOK), BF16),
            pltpu.VMEM((3, HALF, HD), F32),
        ],
        cost_estimate=cost(12 * 16 * TOK * HALF * HD, 8 << 20),
        compiler_params=room(16),
        name="grads",
    )(place, *weights, near, far)


def sum_over_ctx(parts):
    received = {d: shift(parts[d], "x", d, 4) for d in (1, 3, 2)}
    mine = lax.optimization_barrier(add(parts[0], received[1], received[3], received[2]))
    other = shift(mine.astype(BF16), "yh", 1, 2)
    mine = add(mine, other).astype(BF16)
    near = {d: shift(mine, "x", d, 4) for d in (1, 3, 2)}
    pieces = [mine, near[1], near[2], near[3]]
    far = {d: shift(pieces[d], "core", 1, 2) for d in (0, 1, 3, 2)}
    return pieces + [far[d] for d in range(4)]


def apply_kernel(place_ref, high_ref, low_ref, gain_ref, query_ref, *refs):
    outs, trade_ref, (rows_in, rows_out) = refs[:4], refs[4], refs[5:]
    z, yl = place_ref[2], place_ref[3]
    for d in range(4):
        for dy in range(2):
            source = lax.rem(z + 4 - d, 4) * 2 + lax.rem(yl + dy, 2)
            rows_in[pl.ds((d * 2 + dy) * TOK, TOK), :] = query_ref[source]
    gain = gain_ref[...]

    def chunk(step, carry):
        rows = pl.ds(pl.multiple_of(step * 4 * TOK, 4 * TOK), 4 * TOK)
        query = rows_in[rows, :]
        gate = nt(query, high_ref[0]) + nt(query, low_ref[0])
        up = nt(query, high_ref[1]) + nt(query, low_ref[1])
        hidden = (gate * jax.nn.sigmoid(gate) * up).astype(BF16)
        out = nn(hidden, high_ref[2])
        mean = jnp.sum(out * out, axis=1, keepdims=True) * (1.0 / HD)
        rows_out[rows, :] = (out * lax.rsqrt(mean + 1e-5) * gain).astype(BF16)
        return carry

    lax.fori_loop(0, 2, chunk, 0)
    for d in range(4):
        outs[d][...] = rows_out[d * 2 * TOK : (d + 1) * 2 * TOK, :]
        trade_ref[d * TOK : (d + 1) * TOK, :] = rows_out[(2 * d + 1) * TOK : (2 * d + 2) * TOK, :]


def apply_weights(block, place, weights, gain, queries):
    return pl.pallas_call(
        apply_kernel,
        grid=(1,),
        in_specs=[
            SMEM,
            pl.BlockSpec((3, HD, HD), lambda i: (0, 0, 0)),
            pl.BlockSpec((2, HD, HD), lambda i: (0, 0, 0)),
            pl.BlockSpec((1, HD), lambda i: (0, 0)),
            pl.BlockSpec((8, TOK, HD), lambda i: (0, 2 + block, 0)),
        ],
        out_specs=[pl.BlockSpec((2 * TOK, HD), lambda i: (0, 0))] * 4
        + [pl.BlockSpec((4 * TOK, HD), lambda i: (0, 0))],
        out_shape=[jax.ShapeDtypeStruct((2 * TOK, HD), BF16)] * 4
        + [jax.ShapeDtypeStruct((4 * TOK, HD), BF16)],
        scratch_shapes=[pltpu.VMEM((8 * TOK, HD), BF16)] * 2,
        compiler_params=room(16),
        cost_estimate=cost(10 * 8 * TOK * HD * HD, 5 << 20),
        name="apply_weights",
    )(place, *weights, gain, queries)


def project_body(side, place_ref, *refs):
    rows, own, parts = refs[:4], refs[4], refs[5:9]
    keep_ref, send_ref, every, slots, sems = refs[9:]
    step = pl.program_id(0)
    tiles = LONG // TILE
    half = place_ref[0] if side == 0 else 1 - place_ref[0]

    def copies(t):
        slot = lax.rem(t, 2)
        cols = pl.ds(pl.multiple_of(t * TILE, TILE), TILE)
        own_cols = pl.ds(pl.multiple_of(half * COLS + t * TILE, TILE), TILE)
        pairs = [(own.at[:, own_cols], slots.at[slot, pl.ds(0, HD)])]
        for part, start in zip(parts, (HD, 2 * HD, 2 * HD + HALF, 3 * HD)):
            height = part.shape[0]
            pairs.append((part.at[:, cols], slots.at[slot, pl.ds(start, height)]))
        return [
            pltpu.make_async_copy(source, target, sems.at[slot, index])
            for index, (source, target) in enumerate(pairs)
        ]

    @pl.when(step == 0)
    def _():
        for copy in copies(step):
            copy.start()
        for d in range(4):
            every[:, d * HD : (d + 1) * HD] = rows[d][...]

    @pl.when(step + 1 < tiles)
    def _():
        for copy in copies(step + 1):
            copy.start()

    for copy in copies(step):
        copy.wait()
    total = nn(every[...], slots[lax.rem(step, 2)])
    keep_ref[...] = total[:TOK].astype(BF16)
    send_ref[...] = total[TOK:].astype(BF16)


def project(side, place, rows, own, parts):
    tiles = LONG // TILE
    out = pl.BlockSpec((TOK, TILE), lambda t, place_ref: (0, t))
    return pl.pallas_call(
        lambda *refs: project_body(side, *refs),
        grid_spec=pltpu.PrefetchScalarGridSpec(
            num_scalar_prefetch=1,
            grid=(tiles,),
            in_specs=[pl.BlockSpec((2 * TOK, HD), lambda t, place_ref: (0, 0))] * 4
            + [pl.BlockSpec(memory_space=pl.ANY)] * 5,
            out_specs=[out, out],
            scratch_shapes=[
                pltpu.VMEM((2 * TOK, 4 * HD), BF16),
                pltpu.VMEM((2, 4 * HD, TILE), BF16),
                pltpu.SemaphoreType.DMA((2, 5)),
            ],
        ),
        out_shape=[jax.ShapeDtypeStruct((TOK, LONG), BF16)] * 2,
        compiler_params=room(16),
        cost_estimate=cost(2 * 256 * 2560 * LONG, 2560 * LONG * 2),
    )(place, *rows, own, *parts)


def pair_kernel(place_ref, *refs):
    rows, got_ref, own, cross, cross_other = refs[:4], refs[4], refs[5], refs[6], refs[7]
    outs, (every, held, sems) = refs[8:12], refs[12:]
    copies = []
    for side, part in enumerate((cross, cross_other)):
        half = place_ref[0] if side == 0 else 1 - place_ref[0]
        cols = pl.ds(pl.multiple_of(half * COLS + LONG, 512), WIDTH)
        copies.append(
            pltpu.make_async_copy(own.at[:, cols], held.at[side, pl.ds(0, HD)], sems.at[side, 0])
        )
        copies.append(pltpu.make_async_copy(part, held.at[side, pl.ds(HD, HD)], sems.at[side, 1]))
    for copy in copies:
        copy.start()
    for d in range(4):
        every[d * TOK : (d + 1) * TOK, :HD] = rows[d][:TOK, :]
    every[:, HD:] = got_ref[...]
    for copy in copies:
        copy.wait()

    def tile(index, carry):
        side, t = index // 2, lax.rem(index, 2)
        cols = pl.ds(pl.multiple_of(t * 512, 512), 512)
        total = nn(every[...], held[side, :, cols]).astype(BF16)
        out_cols = pl.ds(pl.multiple_of(index * 512, 512), 512)
        for d in range(4):
            outs[d][:, out_cols] = total[d * TOK : (d + 1) * TOK]
        return carry

    lax.fori_loop(0, 4, tile, 0)


def pair_project(place, rows, got, own, cross, cross_other):
    return pl.pallas_call(
        pair_kernel,
        in_specs=[SMEM] + [VMEM] * 5 + [pl.BlockSpec(memory_space=pl.ANY)] * 3,
        out_specs=[VMEM] * 4,
        out_shape=[jax.ShapeDtypeStruct((TOK, 2 * WIDTH), BF16)] * 4,
        scratch_shapes=[
            pltpu.VMEM((4 * TOK, 2 * HD), BF16),
            pltpu.VMEM((2, 2 * HD, WIDTH), BF16),
            pltpu.SemaphoreType.DMA((2, 2)),
        ],
        compiler_params=room(16),
        cost_estimate=cost(2 * 256 * 1280 * 2 * WIDTH, 1280 * 2 * WIDTH * 2),
        name="pair_project",
    )(place, *rows, got, own, cross, cross_other)


def finish_kernel(place_ref, *refs):
    out_ref = refs[-1]
    for block in range(2):
        parts = refs[block * 8 : block * 8 + 8]
        for side in range(2):
            half = place_ref[0] if side == 0 else 1 - place_ref[0]
            start = half * COLS
            total = parts[2 * side][...].astype(F32) + parts[2 * side + 1][...].astype(F32)
            out_ref[block, :, pl.ds(pl.multiple_of(start, 512), LONG)] = total.astype(BF16)
            cols = slice(side * WIDTH, (side + 1) * WIDTH)
            total = parts[4][:, cols].astype(F32)
            for part in parts[5:8]:
                total = total + part[:, cols].astype(F32)
            out_ref[block, :, pl.ds(pl.multiple_of(start + LONG, 512), WIDTH)] = total.astype(BF16)


def finish(place, parts):
    return pl.pallas_call(
        finish_kernel,
        in_specs=[SMEM] + [VMEM] * 16,
        out_specs=VMEM,
        out_shape=jax.ShapeDtypeStruct((2, TOK, WIDE), BF16),
        compiler_params=room(16),
        cost_estimate=cost(1 << 20, 6 << 20),
        name="finish",
    )(place, *parts)


def per_device(queries, keys, values, rates, gate_fast, up_fast, down_fast, out_gain, out_proj):
    core = lax.axis_index("core")
    place = jnp.stack([core] + [lax.axis_index(name) for name in ("x", "z", "yl")])
    place = place.astype(jnp.int32)
    gain = out_gain.reshape(1, HD)
    rates = rates.transpose(0, 2, 1)

    first = to_heads(pack_first(keys, values, rates))
    first_far = shift(first, "core", 1, 2)
    second = to_heads(pack_second(keys, values, rates, queries))
    second_far = shift(second, "core", 1, 2)

    mine = lax.dynamic_slice(out_proj, (0, core * COLS), (HD, LONG))
    slab = lax.dynamic_slice(out_proj, (0, core * COLS + LONG), (HD, WIDTH))
    cross = shift(slab, "yl", 1, 2)
    cross_other = shift(cross, "core", 1, 2)
    before = shift(mine, "z", 1, 4)
    after = shift(mine, "z", 3, 4)
    far_low = shift(before[:HALF], "z", 1, 4)
    far_high = shift(after[HALF:], "z", 3, 4)
    own_side = (before, far_low, far_high, after)
    other_before, other_after = (shift(part, "core", 1, 2) for part in (before, after))
    other_low, other_high = (shift(part, "core", 1, 2) for part in (far_low, far_high))
    other_side = (other_before, other_low, other_high, other_after)

    halves = start_half(place, gate_fast, up_fast, down_fast)
    master, row_norm, col_norm = start_full(gate_fast, up_fast, down_fast)

    def spread(block, weights):
        *rows, trade = apply_weights(block, place, weights, gain, second)
        got = shift(trade, "yl", 1, 2)
        back = {d: shift(rows[d], "z", 4 - d, 4) for d in (2, 1, 3)}
        mine, *others = pair_project(place, rows, got, out_proj, cross, cross_other)
        returned = {d: shift(others[d - 1], "z", 4 - d, 4) for d in (2, 1, 3)}
        ordered = [rows[0], back[3], back[2], back[1]]
        parts = []
        for side, gathered in enumerate((own_side, other_side)):
            keep, send = project(side, place, ordered, out_proj, gathered)
            parts += [keep, shift(send, "yl", 1, 2)]
        return parts + [mine] + [returned[d] for d in (1, 2, 3)]

    total = sum_over_ctx(grads(place, halves, first, first_far))
    weights = renorm(place, [master], row_norm, col_norm, total)
    parts = grads(place, weights, second, second_far)
    total = sum_over_ctx(parts)
    mixed = spread(0, weights)
    weights = renorm(place, weights, row_norm, col_norm, total)
    mixed += spread(1, weights)
    return finish(place, mixed)


def solution(mesh):
    fine = Mesh(mesh.devices.reshape(SIZES), AXES)
    tokens = P(None, AXES, None)
    head = ("z", "yl")
    placed = (
        tokens,
        tokens,
        tokens,
        tokens,
        P(head, None, None),
        P(head, None, None),
        P(head, None, None),
        P(head),
        P(head, None),
    )
    return jax.shard_map(per_device, mesh=fine, in_specs=placed, out_specs=tokens, check_vma=False)
```

```python
import jax
import jax.numpy as jnp
from jax import lax
from jax.experimental import pallas as pl
from jax.experimental.pallas import tpu as pltpu
from jax.sharding import Mesh, PartitionSpec as P

F32 = jnp.float32
BF16 = jnp.bfloat16
AXES = ("x", "yh", "core", "z", "yl")
SIZES = (4, 2, 2, 4, 2)
HD = 640
WIDE = 5120
TOK = 64
HALF = 320
PART = 80
PIECE = 240
COLS = 2560
LONG = 1536
WIDTH = 1024
TILE = 512


VMEM = pl.BlockSpec(memory_space=pltpu.VMEM)
SMEM = pl.BlockSpec(memory_space=pltpu.SMEM)


def cost(flops, moved):
    return pl.CostEstimate(flops=flops, bytes_accessed=moved, transcendentals=0)


def room(mib):
    return pltpu.CompilerParams(vmem_limit_bytes=mib << 20)


def nt(left, right):
    return lax.dot_general(left, right, (((1,), (1,)), ((), ())), preferred_element_type=F32)


def nn(left, right):
    return lax.dot_general(left, right, (((1,), (0,)), ((), ())), preferred_element_type=F32)


def shift(array, axis, by, size):
    return lax.ppermute(array, axis, [(i, (i + by) % size) for i in range(size)])


def to_heads(array):
    return lax.all_to_all(array, ("z", "yl"), 0, 0, tiled=True)


def add(*terms):
    total = terms[0].astype(F32)
    for term in terms[1:]:
        total = total + term.astype(F32)
    return total


def split(matrix):
    high = matrix.astype(BF16)
    return high, (matrix - high.astype(F32)).astype(BF16)


def pack_keys(key_block, value_block, rate_block, out_ref):
    rates = rate_block[0].astype(F32)
    row = lax.broadcasted_iota(jnp.int32, (TOK, TOK), 0)
    lane = lax.broadcasted_iota(jnp.int32, (TOK, TOK), 1)
    for head in range(8):
        cols = slice(head * HD, (head + 1) * HD)
        out_ref[head, :TOK, :] = key_block[0, :, cols]
        spread = jnp.broadcast_to(rates[head : head + 1, :], (TOK, TOK))
        rate = jnp.sum(jnp.where(row == lane, spread, 0.0), axis=1, keepdims=True)
        target = value_block[0, :, cols].astype(F32) * rate
        out_ref[head, TOK : 2 * TOK, :] = target.astype(BF16)


def pack_first_kernel(key_ref, value_ref, rate_ref, out_ref):
    pack_keys(key_ref, value_ref, rate_ref, out_ref)


def pack_second_kernel(key_ref, value_ref, rate_ref, query_ref, out_ref):
    pack_keys(key_ref, value_ref, rate_ref, out_ref)
    for head in range(8):
        for block in range(2):
            start = (2 + block) * TOK
            cols = slice(head * HD, (head + 1) * HD)
            out_ref[head, start : start + TOK, :] = query_ref[block, :, cols]


def block_of(block, width):
    return pl.BlockSpec((1, TOK, width), lambda i: (block, 0, 0))


def rates_of(block):
    return pl.BlockSpec((1, 8, TOK), lambda i: (block, 0, 0))


def pack_first(keys, values, rates):
    return pl.pallas_call(
        pack_first_kernel,
        grid=(1,),
        in_specs=[block_of(0, WIDE), block_of(0, WIDE), rates_of(0)],
        out_specs=pl.BlockSpec((8, 2 * TOK, HD), lambda i: (0, 0, 0)),
        out_shape=jax.ShapeDtypeStruct((8, 2 * TOK, HD), BF16),
        cost_estimate=cost(1 << 20, 4 * TOK * WIDE * 2),
        name="pack_first",
    )(keys, values, rates)


def pack_second(keys, values, rates, queries):
    return pl.pallas_call(
        pack_second_kernel,
        grid=(1,),
        in_specs=[
            block_of(1, WIDE),
            block_of(1, WIDE),
            rates_of(1),
            pl.BlockSpec((2, TOK, WIDE), lambda i: (0, 0, 0)),
        ],
        out_specs=pl.BlockSpec((8, 4 * TOK, HD), lambda i: (0, 0, 0)),
        out_shape=jax.ShapeDtypeStruct((8, 4 * TOK, HD), BF16),
        cost_estimate=cost(1 << 20, 8 * TOK * WIDE * 2),
        name="pack_second",
    )(keys, values, rates, queries)


def start_half_kernel(place_ref, gate_ref, up_ref, down_ref, high_ref, low_ref, loaded, turned, sems):
    core = place_ref[0]
    half = pl.ds(pl.multiple_of(core * HALF, HALF), HALF)
    tiles = pl.ds(pl.multiple_of(core * 256, 256), 384)
    inside = pl.ds(pl.multiple_of(core * (HALF - 256), 64), HALF)
    copies = [
        pltpu.make_async_copy(gate_ref.at[0, :, tiles], loaded.at[0], sems.at[0]),
        pltpu.make_async_copy(up_ref.at[0, :, tiles], loaded.at[1], sems.at[1]),
        pltpu.make_async_copy(down_ref.at[0, half], turned.at[pl.ds(384, HALF)], sems.at[2]),
    ]
    for copy in copies:
        copy.start()
    for slot in range(2):
        copies[slot].wait()
        turned[:384, :] = loaded[slot].T
        high_ref[slot], low_ref[slot] = split(turned[inside, :])
    copies[2].wait()
    high_ref[2], low_ref[2] = split(turned[384:, :])


def start_half(place, gate, up, down):
    return pl.pallas_call(
        start_half_kernel,
        in_specs=[SMEM] + [pl.BlockSpec(memory_space=pltpu.HBM)] * 3,
        out_specs=[VMEM] * 2,
        out_shape=[jax.ShapeDtypeStruct((3, HALF, HD), BF16)] * 2,
        scratch_shapes=[
            pltpu.VMEM((2, HD, 384), F32),
            pltpu.VMEM((384 + HALF, HD), F32),
            pltpu.SemaphoreType.DMA((3,)),
        ],
        compiler_params=room(16),
        cost_estimate=cost(1 << 24, 3 * HD * HD * 6),
        name="start_half",
    )(place, gate, up, down)


def start_full_kernel(gate_ref, up_ref, down_ref, master_ref, row_norm_ref, col_norm_ref):
    for slot, ref in ((0, gate_ref), (1, up_ref)):
        matrix = ref[0].T
        master_ref[slot] = matrix
        row_norm_ref[slot] = jnp.sqrt(jnp.sum(matrix * matrix, axis=1, keepdims=True))
    matrix = down_ref[0]
    master_ref[2] = matrix
    col_norm_ref[...] = jnp.sqrt(jnp.sum(matrix * matrix, axis=0, keepdims=True))


def start_full(gate, up, down):
    return pl.pallas_call(
        start_full_kernel,
        in_specs=[VMEM] * 3,
        out_specs=[VMEM] * 3,
        out_shape=[
            pltpu.VMEM((3, HD, HD), F32),
            pltpu.VMEM((2, HD, 1), F32),
            pltpu.VMEM((1, HD), F32),
        ],
        compiler_params=room(16),
        cost_estimate=cost(1 << 24, 3 * HD * HD * 8),
        name="start_full",
    )(gate, up, down)


def renorm_kernel(count, place_ref, *refs):
    old_refs, (row_norm_ref, col_norm_ref) = refs[:count], refs[count : count + 2]
    pieces, outs, down_ref = refs[count + 2 : count + 10], refs[count + 10 : -1], refs[-1]
    core, x = place_ref[0], place_ref[1]
    squares = jnp.zeros((8, HD), F32)

    def store(where, matrix):
        for out, part in zip(outs, split(matrix)):
            out[where] = part

    def moved_rows(slot, rows, step):
        total = step.astype(F32)
        for old_ref in old_refs:
            total = total + old_ref[slot, rows, :].astype(F32)
        return total

    for index, piece in enumerate(pieces):
        side, d = index // 4, index % 4
        owner = core if side == 0 else 1 - core
        start = pl.multiple_of(owner * HALF + lax.rem(x + 4 - d, 4) * PART, 16)
        rows = pl.ds(start, PART)
        for slot in range(2):
            moved = moved_rows(slot, rows, piece[slot * PART : (slot + 1) * PART, :])
            scale = row_norm_ref[slot, rows, :] * lax.rsqrt(
                jnp.sum(moved * moved, axis=1, keepdims=True) + 1e-6
            )
            store((slot, rows, slice(None)), moved * scale)
        moved = moved_rows(2, rows, piece[2 * PART :, :])
        down_ref[rows, :] = moved
        squares = squares + jnp.sum((moved * moved).reshape(PART // 8, 8, HD), axis=0)
    scale = col_norm_ref[...] * lax.rsqrt(jnp.sum(squares, axis=0, keepdims=True) + 1e-6)
    store(2, down_ref[...] * scale)


def renorm(place, weights, row_norm, col_norm, pieces, last=False):
    return pl.pallas_call(
        lambda *refs: renorm_kernel(len(weights), *refs),
        in_specs=[SMEM] + [VMEM] * (10 + len(weights)),
        out_specs=[VMEM] * (1 if last else 2),
        out_shape=[pltpu.VMEM((3, HD, HD), BF16)] * (1 if last else 2),
        scratch_shapes=[pltpu.VMEM((HD, HD), F32)],
        compiler_params=room(16),
        cost_estimate=cost(1 << 24, 3 * HD * HD * 10),
        name="renorm",
    )(place, *weights, row_norm, col_norm, *pieces)


def grads_kernel(place_ref, high_ref, low_ref, near_ref, far_ref, *refs):
    outs, (tokens, inner, total), loaded = refs[:4], refs[4:7], refs[7:]
    core, x = place_ref[0], place_ref[1]
    copies = []
    if loaded:
        held, sems = loaded
        copies = [
            pltpu.make_async_copy(ref, held.at[index], sems.at[index])
            for index, ref in enumerate((high_ref, low_ref))
        ]
        high_ref, low_ref = held.at[0], held.at[1]
    for copy in copies:
        copy.start()
    for side, ref in enumerate((near_ref, far_ref)):
        for index in range(8):
            rows = pl.ds((side * 8 + index) * TOK, TOK)
            tokens[0, rows, :] = ref[index, :TOK, :]
            tokens[1, rows, :] = ref[index, TOK : 2 * TOK, :]
    for copy in copies:
        copy.wait()
    height = high_ref.shape[1]
    half = pl.ds(pl.multiple_of(core * (height - HALF), HALF), HALF)

    def product(slot, rows):
        return nt(high_ref[slot, half, :], rows) + nt(low_ref[slot, half, :], rows)

    def chunk(step, carry):
        rows = pl.ds(pl.multiple_of(step * 256, 256), 256)
        key = tokens[0, rows, :]
        gate = product(0, key)
        up = product(1, key)
        back = product(2, tokens[1, rows, :])
        sigma = jax.nn.sigmoid(gate)
        silu = gate * sigma
        inner[0, :, rows] = (back * up * sigma * (1.0 + gate * (1.0 - sigma))).astype(BF16)
        inner[1, :, rows] = (back * silu).astype(BF16)
        inner[2, :, rows] = (silu * up).astype(BF16)
        return carry

    lax.fori_loop(0, 4, chunk, 0)

    def finish(slot, carry):
        total[slot] = nn(inner[slot], tokens[slot // 2])
        return carry

    lax.fori_loop(0, 3, finish, 0)
    for d in range(4):
        rows = pl.ds(pl.multiple_of(lax.rem(x + d, 4) * PART, 16), PART)
        for slot in range(3):
            outs[d][slot * PART : (slot + 1) * PART, :] = total[slot, rows, :].astype(outs[d].dtype)


def grads(place, weights, near, far):
    part = pl.BlockSpec((8, 2 * TOK, HD), lambda i: (0, 0, 0))
    held = pl.BlockSpec(weights[0].shape, lambda i: (0, 0, 0))
    extra = []
    if weights[0].shape[1] == HALF:
        held = pl.BlockSpec(memory_space=pltpu.HBM)
        extra = [pltpu.VMEM((2, 3, HALF, HD), BF16), pltpu.SemaphoreType.DMA((2,))]
    return pl.pallas_call(
        grads_kernel,
        grid=(1,),
        in_specs=[SMEM] + [held] * 2 + [part] * 2,
        out_specs=[pl.BlockSpec((PIECE, HD), lambda i: (0, 0))] * 4,
        out_shape=[pltpu.VMEM((PIECE, HD), F32 if d == 0 else BF16) for d in range(4)],
        scratch_shapes=[
            pltpu.VMEM((2, 16 * TOK, HD), BF16),
            pltpu.VMEM((3, HALF, 16 * TOK), BF16),
            pltpu.VMEM((3, HALF, HD), F32),
        ]
        + extra,
        cost_estimate=cost(12 * 16 * TOK * HALF * HD, 8 << 20),
        compiler_params=None if extra else room(20),
        name="grads",
    )(place, *weights, near, far)


def sum_over_ctx(parts):
    received = {d: shift(parts[d], "x", d, 4) for d in (1, 3, 2)}
    mine = lax.optimization_barrier(add(parts[0], received[1], received[3], received[2]))
    other = shift(mine.astype(BF16), "yh", 1, 2)
    mine = add(mine, other).astype(BF16)
    near = {d: shift(mine, "x", d, 4) for d in (1, 3, 2)}
    pieces = [mine, near[1], near[2], near[3]]
    far = {d: shift(pieces[d], "core", 1, 2) for d in (0, 1, 3, 2)}
    return pieces + [far[d] for d in range(4)]


def apply_kernel(place_ref, high_ref, gain_ref, query_ref, *refs):
    outs, trade_ref, (rows_in, rows_out) = refs[:4], refs[4], refs[5:]
    z, yl = place_ref[2], place_ref[3]
    for d in range(4):
        for dy in range(2):
            source = lax.rem(z + 4 - d, 4) * 2 + lax.rem(yl + dy, 2)
            rows_in[pl.ds((d * 2 + dy) * TOK, TOK), :] = query_ref[source]
    gain = gain_ref[...]

    def chunk(step, carry):
        rows = pl.ds(pl.multiple_of(step * 4 * TOK, 4 * TOK), 4 * TOK)
        query = rows_in[rows, :]
        gate = nt(query, high_ref[0])
        up = nt(query, high_ref[1])
        hidden = (gate * jax.nn.sigmoid(gate) * up).astype(BF16)
        out = nn(hidden, high_ref[2])
        mean = jnp.sum(out * out, axis=1, keepdims=True) * (1.0 / HD)
        rows_out[rows, :] = (out * lax.rsqrt(mean + 1e-5) * gain).astype(BF16)
        return carry

    lax.fori_loop(0, 2, chunk, 0)
    for d in range(4):
        outs[d][...] = rows_out[d * 2 * TOK : (d + 1) * 2 * TOK, :]
        trade_ref[d * TOK : (d + 1) * TOK, :] = rows_out[(2 * d + 1) * TOK : (2 * d + 2) * TOK, :]


def apply_weights(block, place, weights, gain, queries):
    return pl.pallas_call(
        apply_kernel,
        grid=(1,),
        in_specs=[
            SMEM,
            pl.BlockSpec((3, HD, HD), lambda i: (0, 0, 0)),
            pl.BlockSpec((1, HD), lambda i: (0, 0)),
            pl.BlockSpec((8, TOK, HD), lambda i: (0, 2 + block, 0)),
        ],
        out_specs=[pl.BlockSpec((2 * TOK, HD), lambda i: (0, 0))] * 4
        + [pl.BlockSpec((4 * TOK, HD), lambda i: (0, 0))],
        out_shape=[jax.ShapeDtypeStruct((2 * TOK, HD), BF16)] * 4
        + [jax.ShapeDtypeStruct((4 * TOK, HD), BF16)],
        scratch_shapes=[pltpu.VMEM((8 * TOK, HD), BF16)] * 2,
        compiler_params=room(16),
        cost_estimate=cost(6 * 8 * TOK * HD * HD, 5 << 20),
        name="apply_weights",
    )(place, weights[0], gain, queries)


def project_body(side, place_ref, *refs):
    rows, own, parts = refs[:4], refs[4], refs[5:9]
    keep_ref, send_ref, every, slots, sems = refs[9:]
    step = pl.program_id(0)
    tiles = LONG // TILE
    half = place_ref[0] if side == 0 else 1 - place_ref[0]

    def copies(t):
        slot = lax.rem(t, 2)
        cols = pl.ds(pl.multiple_of(t * TILE, TILE), TILE)
        own_cols = pl.ds(pl.multiple_of(half * COLS + t * TILE, TILE), TILE)
        pairs = [(own.at[:, own_cols], slots.at[slot, pl.ds(0, HD)])]
        for part, start in zip(parts, (HD, 2 * HD, 2 * HD + HALF, 3 * HD)):
            height = part.shape[0]
            pairs.append((part.at[:, cols], slots.at[slot, pl.ds(start, height)]))
        return [
            pltpu.make_async_copy(source, target, sems.at[slot, index])
            for index, (source, target) in enumerate(pairs)
        ]

    @pl.when(step == 0)
    def _():
        for copy in copies(step):
            copy.start()
        for d in range(4):
            every[:, d * HD : (d + 1) * HD] = rows[d][...]

    @pl.when(step + 1 < tiles)
    def _():
        for copy in copies(step + 1):
            copy.start()

    for copy in copies(step):
        copy.wait()
    total = nn(every[...], slots[lax.rem(step, 2)])
    keep_ref[...] = total[:TOK].astype(BF16)
    send_ref[...] = total[TOK:].astype(BF16)


def project(side, place, rows, own, parts):
    tiles = LONG // TILE
    out = pl.BlockSpec((TOK, TILE), lambda t, place_ref: (0, t))
    return pl.pallas_call(
        lambda *refs: project_body(side, *refs),
        grid_spec=pltpu.PrefetchScalarGridSpec(
            num_scalar_prefetch=1,
            grid=(tiles,),
            in_specs=[pl.BlockSpec((2 * TOK, HD), lambda t, place_ref: (0, 0))] * 4
            + [pl.BlockSpec(memory_space=pl.ANY)] * 5,
            out_specs=[out, out],
            scratch_shapes=[
                pltpu.VMEM((2 * TOK, 4 * HD), BF16),
                pltpu.VMEM((2, 4 * HD, TILE), BF16),
                pltpu.SemaphoreType.DMA((2, 5)),
            ],
        ),
        out_shape=[jax.ShapeDtypeStruct((TOK, LONG), BF16)] * 2,
        compiler_params=room(16),
        cost_estimate=cost(2 * 256 * 2560 * LONG, 2560 * LONG * 2),
    )(place, *rows, own, *parts)


def pair_kernel(place_ref, *refs):
    rows, got_ref, own, cross, cross_other = refs[:4], refs[4], refs[5], refs[6], refs[7]
    outs, (every, held, sems) = refs[8:12], refs[12:]
    copies = []
    for side, part in enumerate((cross, cross_other)):
        half = place_ref[0] if side == 0 else 1 - place_ref[0]
        cols = pl.ds(pl.multiple_of(half * COLS + LONG, 512), WIDTH)
        copies.append(
            pltpu.make_async_copy(own.at[:, cols], held.at[side, pl.ds(0, HD)], sems.at[side, 0])
        )
        copies.append(pltpu.make_async_copy(part, held.at[side, pl.ds(HD, HD)], sems.at[side, 1]))
    for copy in copies:
        copy.start()
    for d in range(4):
        every[d * TOK : (d + 1) * TOK, :HD] = rows[d][:TOK, :]
    every[:, HD:] = got_ref[...]
    for copy in copies:
        copy.wait()

    def tile(index, carry):
        side, t = index // 2, lax.rem(index, 2)
        cols = pl.ds(pl.multiple_of(t * 512, 512), 512)
        total = nn(every[...], held[side, :, cols]).astype(BF16)
        out_cols = pl.ds(pl.multiple_of(index * 512, 512), 512)
        for d in range(4):
            outs[d][:, out_cols] = total[d * TOK : (d + 1) * TOK]
        return carry

    lax.fori_loop(0, 4, tile, 0)


def pair_project(place, rows, got, own, cross, cross_other):
    return pl.pallas_call(
        pair_kernel,
        in_specs=[SMEM] + [VMEM] * 5 + [pl.BlockSpec(memory_space=pl.ANY)] * 3,
        out_specs=[VMEM] * 4,
        out_shape=[jax.ShapeDtypeStruct((TOK, 2 * WIDTH), BF16)] * 4,
        scratch_shapes=[
            pltpu.VMEM((4 * TOK, 2 * HD), BF16),
            pltpu.VMEM((2, 2 * HD, WIDTH), BF16),
            pltpu.SemaphoreType.DMA((2, 2)),
        ],
        compiler_params=room(16),
        cost_estimate=cost(2 * 256 * 1280 * 2 * WIDTH, 1280 * 2 * WIDTH * 2),
        name="pair_project",
    )(place, *rows, got, own, cross, cross_other)


def finish_kernel(place_ref, *refs):
    parts, out_ref = refs[:8], refs[-1]
    for side in range(2):
        half = place_ref[0] if side == 0 else 1 - place_ref[0]
        start = half * COLS
        total = parts[2 * side][...].astype(F32) + parts[2 * side + 1][...].astype(F32)
        out_ref[0, :, pl.ds(pl.multiple_of(start, 512), LONG)] = total.astype(BF16)
        cols = slice(side * WIDTH, (side + 1) * WIDTH)
        total = parts[4][:, cols].astype(F32)
        for part in parts[5:8]:
            total = total + part[:, cols].astype(F32)
        out_ref[0, :, pl.ds(pl.multiple_of(start + LONG, 512), WIDTH)] = total.astype(BF16)


def finish(block, place, parts, held=None):
    held = [] if held is None else [held]
    whole = [pl.BlockSpec(part.shape, lambda i: (0, 0)) for part in parts]
    return pl.pallas_call(
        finish_kernel,
        grid=(1,),
        in_specs=[SMEM] + whole + [pl.BlockSpec(memory_space=pl.ANY)] * len(held),
        out_specs=pl.BlockSpec((1, TOK, WIDE), lambda i: (block, 0, 0)),
        out_shape=jax.ShapeDtypeStruct((2, TOK, WIDE), BF16),
        input_output_aliases={9: 0} if held else {},
        compiler_params=room(16),
        cost_estimate=cost(1 << 20, 3 << 20),
        name="finish",
    )(place, *parts, *held)


def per_device(queries, keys, values, rates, gate_fast, up_fast, down_fast, out_gain, out_proj):
    core = lax.axis_index("core")
    place = jnp.stack([core] + [lax.axis_index(name) for name in ("x", "z", "yl")])
    place = place.astype(jnp.int32)
    gain = out_gain.reshape(1, HD)
    rates = rates.transpose(0, 2, 1)

    first = to_heads(pack_first(keys, values, rates))
    first_far = shift(first, "core", 1, 2)
    second = to_heads(pack_second(keys, values, rates, queries))
    second_far = shift(second, "core", 1, 2)

    mine = lax.dynamic_slice(out_proj, (0, core * COLS), (HD, LONG))
    slab = lax.dynamic_slice(out_proj, (0, core * COLS + LONG), (HD, WIDTH))
    cross = shift(slab, "yl", 1, 2)
    cross_other = shift(cross, "core", 1, 2)
    before = shift(mine, "z", 1, 4)
    after = shift(mine, "z", 3, 4)
    far_low = shift(before[:HALF], "z", 1, 4)
    far_high = shift(after[HALF:], "z", 3, 4)
    own_side = (before, far_low, far_high, after)
    other_before, other_after = (shift(part, "core", 1, 2) for part in (before, after))
    other_low, other_high = (shift(part, "core", 1, 2) for part in (far_low, far_high))
    other_side = (other_before, other_low, other_high, other_after)

    halves = start_half(place, gate_fast, up_fast, down_fast)
    master, row_norm, col_norm = start_full(gate_fast, up_fast, down_fast)

    def spread(block, weights):
        *rows, trade = apply_weights(block, place, weights, gain, second)
        got = shift(trade, "yl", 1, 2)
        back = {d: shift(rows[d], "z", 4 - d, 4) for d in (2, 1, 3)}
        mine, *others = pair_project(place, rows, got, out_proj, cross, cross_other)
        returned = {d: shift(others[d - 1], "z", 4 - d, 4) for d in (2, 1, 3)}
        ordered = [rows[0], back[3], back[2], back[1]]
        parts = []
        for side, gathered in enumerate((own_side, other_side)):
            keep, send = project(side, place, ordered, out_proj, gathered)
            parts += [keep, shift(send, "yl", 1, 2)]
        return parts + [mine] + [returned[d] for d in (1, 2, 3)]

    total = sum_over_ctx(grads(place, halves, first, first_far))
    weights = renorm(place, [master], row_norm, col_norm, total)
    parts = grads(place, weights, second, second_far)
    total = sum_over_ctx(parts)
    parts = spread(0, weights)
    out = finish(0, place, parts)
    weights = renorm(place, weights, row_norm, col_norm, total, True)
    return finish(1, place, spread(1, weights), out)


def solution(mesh):
    fine = Mesh(mesh.devices.reshape(SIZES), AXES)
    tokens = P(None, AXES, None)
    head = ("z", "yl")
    placed = (
        tokens,
        tokens,
        tokens,
        tokens,
        P(head, None, None),
        P(head, None, None),
        P(head, None, None),
        P(head),
        P(head, None),
    )
    return jax.shard_map(per_device, mesh=fine, in_specs=placed, out_specs=tokens, check_vma=False)
```

```python
import jax
import jax.numpy as jnp
from jax import lax
from jax.experimental import pallas as pl
from jax.experimental.pallas import tpu as pltpu
from jax.sharding import Mesh, PartitionSpec as P

F32 = jnp.float32
BF16 = jnp.bfloat16
AXES = ("x", "yh", "core", "z", "yl")
SIZES = (4, 2, 2, 4, 2)
HD = 640
WIDE = 5120
TOK = 64
HALF = 320
PART = 80
PIECE = 240
COLS = 2560
LONG = 1536
WIDTH = 1024
TILE = 512


VMEM = pl.BlockSpec(memory_space=pltpu.VMEM)
SMEM = pl.BlockSpec(memory_space=pltpu.SMEM)


def cost(flops, moved):
    return pl.CostEstimate(flops=flops, bytes_accessed=moved, transcendentals=0)


def room(mib):
    return pltpu.CompilerParams(vmem_limit_bytes=mib << 20)


def nt(left, right):
    return lax.dot_general(left, right, (((1,), (1,)), ((), ())), preferred_element_type=F32)


def nn(left, right):
    return lax.dot_general(left, right, (((1,), (0,)), ((), ())), preferred_element_type=F32)


def shift(array, axis, by, size):
    return lax.ppermute(array, axis, [(i, (i + by) % size) for i in range(size)])


def to_heads(array):
    return lax.all_to_all(array, ("z", "yl"), 0, 0, tiled=True)


def add(*terms):
    total = terms[0].astype(F32)
    for term in terms[1:]:
        total = total + term.astype(F32)
    return total


def split(matrix):
    high = matrix.astype(BF16)
    return high, (matrix - high.astype(F32)).astype(BF16)


def pack_keys(key_block, value_block, rate_block, out_ref):
    rates = rate_block[0].astype(F32)
    row = lax.broadcasted_iota(jnp.int32, (TOK, TOK), 0)
    lane = lax.broadcasted_iota(jnp.int32, (TOK, TOK), 1)
    for head in range(8):
        cols = slice(head * HD, (head + 1) * HD)
        out_ref[head, :TOK, :] = key_block[0, :, cols]
        spread = jnp.broadcast_to(rates[head : head + 1, :], (TOK, TOK))
        rate = jnp.sum(jnp.where(row == lane, spread, 0.0), axis=1, keepdims=True)
        target = value_block[0, :, cols].astype(F32) * rate
        out_ref[head, TOK : 2 * TOK, :] = target.astype(BF16)


def pack_first_kernel(key_ref, value_ref, rate_ref, out_ref):
    pack_keys(key_ref, value_ref, rate_ref, out_ref)


def pack_second_kernel(key_ref, value_ref, rate_ref, query_ref, out_ref):
    pack_keys(key_ref, value_ref, rate_ref, out_ref)
    for head in range(8):
        for block in range(2):
            start = (2 + block) * TOK
            cols = slice(head * HD, (head + 1) * HD)
            out_ref[head, start : start + TOK, :] = query_ref[block, :, cols]


def block_of(block, width):
    return pl.BlockSpec((1, TOK, width), lambda i: (block, 0, 0))


def rates_of(block):
    return pl.BlockSpec((1, 8, TOK), lambda i: (block, 0, 0))


def pack_first(keys, values, rates):
    return pl.pallas_call(
        pack_first_kernel,
        grid=(1,),
        in_specs=[block_of(0, WIDE), block_of(0, WIDE), rates_of(0)],
        out_specs=pl.BlockSpec((8, 2 * TOK, HD), lambda i: (0, 0, 0)),
        out_shape=jax.ShapeDtypeStruct((8, 2 * TOK, HD), BF16),
        cost_estimate=cost(1 << 20, 4 * TOK * WIDE * 2),
        name="pack_first",
    )(keys, values, rates)


def pack_second(keys, values, rates, queries):
    return pl.pallas_call(
        pack_second_kernel,
        grid=(1,),
        in_specs=[
            block_of(1, WIDE),
            block_of(1, WIDE),
            rates_of(1),
            pl.BlockSpec((2, TOK, WIDE), lambda i: (0, 0, 0)),
        ],
        out_specs=pl.BlockSpec((8, 4 * TOK, HD), lambda i: (0, 0, 0)),
        out_shape=jax.ShapeDtypeStruct((8, 4 * TOK, HD), BF16),
        cost_estimate=cost(1 << 20, 8 * TOK * WIDE * 2),
        name="pack_second",
    )(keys, values, rates, queries)


def start_half_kernel(place_ref, gate_ref, up_ref, down_ref, high_ref, low_ref, loaded, turned, sems):
    core = place_ref[0]
    half = pl.ds(pl.multiple_of(core * HALF, HALF), HALF)
    tiles = pl.ds(pl.multiple_of(core * 256, 256), 384)
    inside = pl.ds(pl.multiple_of(core * (HALF - 256), 64), HALF)
    copies = [
        pltpu.make_async_copy(gate_ref.at[0, :, tiles], loaded.at[0], sems.at[0]),
        pltpu.make_async_copy(up_ref.at[0, :, tiles], loaded.at[1], sems.at[1]),
        pltpu.make_async_copy(down_ref.at[0, half], turned.at[pl.ds(384, HALF)], sems.at[2]),
    ]
    for copy in copies:
        copy.start()
    for slot in range(2):
        copies[slot].wait()
        turned[:384, :] = loaded[slot].T
        high_ref[slot], low_ref[slot] = split(turned[inside, :])
    copies[2].wait()
    high_ref[2], low_ref[2] = split(turned[384:, :])


def start_half(place, gate, up, down):
    return pl.pallas_call(
        start_half_kernel,
        in_specs=[SMEM] + [pl.BlockSpec(memory_space=pltpu.HBM)] * 3,
        out_specs=[VMEM] * 2,
        out_shape=[jax.ShapeDtypeStruct((3, HALF, HD), BF16)] * 2,
        scratch_shapes=[
            pltpu.VMEM((2, HD, 384), F32),
            pltpu.VMEM((384 + HALF, HD), F32),
            pltpu.SemaphoreType.DMA((3,)),
        ],
        compiler_params=room(16),
        cost_estimate=cost(1 << 24, 3 * HD * HD * 6),
        name="start_half",
    )(place, gate, up, down)


def start_full_kernel(gate_ref, up_ref, down_ref, master_ref, row_norm_ref, col_norm_ref):
    for slot, ref in ((0, gate_ref), (1, up_ref)):
        matrix = ref[0].T
        master_ref[slot] = matrix
        row_norm_ref[slot] = jnp.sqrt(jnp.sum(matrix * matrix, axis=1, keepdims=True))
    matrix = down_ref[0]
    master_ref[2] = matrix
    col_norm_ref[...] = jnp.sqrt(jnp.sum(matrix * matrix, axis=0, keepdims=True))


def start_full(gate, up, down):
    return pl.pallas_call(
        start_full_kernel,
        in_specs=[VMEM] * 3,
        out_specs=[VMEM] * 3,
        out_shape=[
            pltpu.VMEM((3, HD, HD), F32),
            pltpu.VMEM((2, HD, 1), F32),
            pltpu.VMEM((1, HD), F32),
        ],
        compiler_params=room(16),
        cost_estimate=cost(1 << 24, 3 * HD * HD * 8),
        name="start_full",
    )(gate, up, down)


def renorm_kernel(count, place_ref, *refs):
    old_refs, (row_norm_ref, col_norm_ref) = refs[:count], refs[count : count + 2]
    pieces, outs, down_ref = refs[count + 2 : count + 10], refs[count + 10 : -1], refs[-1]
    core, x = place_ref[0], place_ref[1]
    squares = jnp.zeros((8, HD), F32)

    def store(where, matrix):
        for out, part in zip(outs, split(matrix)):
            out[where] = part

    def moved_rows(slot, rows, step):
        total = step.astype(F32)
        for old_ref in old_refs:
            total = total + old_ref[slot, rows, :].astype(F32)
        return total

    for index, piece in enumerate(pieces):
        side, d = index // 4, index % 4
        owner = core if side == 0 else 1 - core
        start = pl.multiple_of(owner * HALF + lax.rem(x + 4 - d, 4) * PART, 16)
        rows = pl.ds(start, PART)
        for slot in range(2):
            moved = moved_rows(slot, rows, piece[slot * PART : (slot + 1) * PART, :])
            scale = row_norm_ref[slot, rows, :] * lax.rsqrt(
                jnp.sum(moved * moved, axis=1, keepdims=True) + 1e-6
            )
            store((slot, rows, slice(None)), moved * scale)
        moved = moved_rows(2, rows, piece[2 * PART :, :])
        down_ref[rows, :] = moved
        squares = squares + jnp.sum((moved * moved).reshape(PART // 8, 8, HD), axis=0)
    scale = col_norm_ref[...] * lax.rsqrt(jnp.sum(squares, axis=0, keepdims=True) + 1e-6)
    store(2, down_ref[...] * scale)


def renorm(place, weights, row_norm, col_norm, pieces, last=False):
    return pl.pallas_call(
        lambda *refs: renorm_kernel(len(weights), *refs),
        in_specs=[SMEM] + [VMEM] * (10 + len(weights)),
        out_specs=[VMEM] * (1 if last else 2),
        out_shape=[pltpu.VMEM((3, HD, HD), BF16)] * (1 if last else 2),
        scratch_shapes=[pltpu.VMEM((HD, HD), F32)],
        compiler_params=room(16),
        cost_estimate=cost(1 << 24, 3 * HD * HD * 10),
        name="renorm",
    )(place, *weights, row_norm, col_norm, *pieces)


def grads_kernel(place_ref, high_ref, low_ref, near_ref, far_ref, *refs):
    outs, (inner, total), loaded = refs[:4], refs[4:6], refs[6:]
    core, x = place_ref[0], place_ref[1]
    copies = []
    if loaded:
        held, sems = loaded
        copies = [
            pltpu.make_async_copy(ref, held.at[index], sems.at[index])
            for index, ref in enumerate((high_ref, low_ref))
        ]
        high_ref, low_ref = held.at[0], held.at[1]
    for copy in copies:
        copy.start()
    for copy in copies:
        copy.wait()
    height = high_ref.shape[1]
    half = pl.ds(pl.multiple_of(core * (height - HALF), HALF), HALF)

    def product(slot, rows):
        return nt(high_ref[slot, half, :], rows) + nt(low_ref[slot, half, :], rows)

    for side, ref in enumerate((near_ref, far_ref)):

        def chunk(step, carry, side=side, ref=ref):
            four = pl.ds(step * 4, 4)
            rows = pl.ds(pl.multiple_of(side * 512 + step * 256, 256), 256)
            key = ref[four, :TOK, :].reshape(4 * TOK, HD)
            gate = product(0, key)
            up = product(1, key)
            back = product(2, ref[four, TOK : 2 * TOK, :].reshape(4 * TOK, HD))
            sigma = jax.nn.sigmoid(gate)
            silu = gate * sigma
            inner[0, :, rows] = (back * up * sigma * (1.0 + gate * (1.0 - sigma))).astype(BF16)
            inner[1, :, rows] = (back * silu).astype(BF16)
            inner[2, :, rows] = (silu * up).astype(BF16)
            return carry

        lax.fori_loop(0, 2, chunk, 0)

    def finish(slot, carry):
        kind = pl.ds(pl.multiple_of(slot // 2 * TOK, TOK), TOK)
        near = nn(inner[slot, :, :512], near_ref[:, kind, :].reshape(8 * TOK, HD))
        far = nn(inner[slot, :, 512:], far_ref[:, kind, :].reshape(8 * TOK, HD))
        total[slot] = near + far
        return carry

    lax.fori_loop(0, 3, finish, 0)
    for d in range(4):
        rows = pl.ds(pl.multiple_of(lax.rem(x + d, 4) * PART, 16), PART)
        for slot in range(3):
            outs[d][slot * PART : (slot + 1) * PART, :] = total[slot, rows, :].astype(outs[d].dtype)


def grads(place, weights, near, far):
    part = pl.BlockSpec((8, 2 * TOK, HD), lambda i: (0, 0, 0))
    held = pl.BlockSpec(weights[0].shape, lambda i: (0, 0, 0))
    extra = []
    if weights[0].shape[1] == HALF:
        held = pl.BlockSpec(memory_space=pltpu.HBM)
        extra = [pltpu.VMEM((2, 3, HALF, HD), BF16), pltpu.SemaphoreType.DMA((2,))]
    return pl.pallas_call(
        grads_kernel,
        grid=(1,),
        in_specs=[SMEM] + [held] * 2 + [part] * 2,
        out_specs=[pl.BlockSpec((PIECE, HD), lambda i: (0, 0))] * 4,
        out_shape=[pltpu.VMEM((PIECE, HD), F32 if d == 0 else BF16) for d in range(4)],
        scratch_shapes=[
            pltpu.VMEM((3, HALF, 16 * TOK), BF16),
            pltpu.VMEM((3, HALF, HD), F32),
        ]
        + extra,
        cost_estimate=cost(12 * 16 * TOK * HALF * HD, 8 << 20),
        compiler_params=None if extra else room(20),
        name="grads",
    )(place, *weights, near, far)


def sum_over_ctx(parts):
    received = {d: shift(parts[d], "x", d, 4) for d in (1, 3, 2)}
    mine = lax.optimization_barrier(add(parts[0], received[1], received[3], received[2]))
    other = shift(mine.astype(BF16), "yh", 1, 2)
    mine = add(mine, other).astype(BF16)
    near = {d: shift(mine, "x", d, 4) for d in (1, 3, 2)}
    pieces = [mine, near[1], near[2], near[3]]
    far = {d: shift(pieces[d], "core", 1, 2) for d in (0, 1, 3, 2)}
    return pieces + [far[d] for d in range(4)]


def apply_kernel(place_ref, high_ref, gain_ref, query_ref, *refs):
    outs, trade_ref, (rows_in, rows_out) = refs[:4], refs[4], refs[5:]
    z, yl = place_ref[2], place_ref[3]
    for d in range(4):
        for dy in range(2):
            source = lax.rem(z + 4 - d, 4) * 2 + lax.rem(yl + dy, 2)
            rows_in[pl.ds((d * 2 + dy) * TOK, TOK), :] = query_ref[source]
    gain = gain_ref[...]

    def chunk(step, carry):
        rows = pl.ds(pl.multiple_of(step * 4 * TOK, 4 * TOK), 4 * TOK)
        query = rows_in[rows, :]
        gate = nt(query, high_ref[0])
        up = nt(query, high_ref[1])
        hidden = (gate * jax.nn.sigmoid(gate) * up).astype(BF16)
        out = nn(hidden, high_ref[2])
        mean = jnp.sum(out * out, axis=1, keepdims=True) * (1.0 / HD)
        rows_out[rows, :] = (out * lax.rsqrt(mean + 1e-5) * gain).astype(BF16)
        return carry

    lax.fori_loop(0, 2, chunk, 0)
    for d in range(4):
        outs[d][...] = rows_out[d * 2 * TOK : (d + 1) * 2 * TOK, :]
        trade_ref[d * TOK : (d + 1) * TOK, :] = rows_out[(2 * d + 1) * TOK : (2 * d + 2) * TOK, :]


def apply_weights(block, place, weights, gain, queries):
    return pl.pallas_call(
        apply_kernel,
        grid=(1,),
        in_specs=[
            SMEM,
            pl.BlockSpec((3, HD, HD), lambda i: (0, 0, 0)),
            pl.BlockSpec((1, HD), lambda i: (0, 0)),
            pl.BlockSpec((8, TOK, HD), lambda i: (0, 2 + block, 0)),
        ],
        out_specs=[pl.BlockSpec((2 * TOK, HD), lambda i: (0, 0))] * 4
        + [pl.BlockSpec((4 * TOK, HD), lambda i: (0, 0))],
        out_shape=[jax.ShapeDtypeStruct((2 * TOK, HD), BF16)] * 4
        + [jax.ShapeDtypeStruct((4 * TOK, HD), BF16)],
        scratch_shapes=[pltpu.VMEM((8 * TOK, HD), BF16)] * 2,
        compiler_params=room(16),
        cost_estimate=cost(6 * 8 * TOK * HD * HD, 5 << 20),
        name="apply_weights",
    )(place, weights[0], gain, queries)


def project_body(side, place_ref, *refs):
    rows, own, parts = refs[:4], refs[4], refs[5:9]
    keep_ref, send_ref, every, slots, sems = refs[9:]
    step = pl.program_id(0)
    tiles = LONG // TILE
    half = place_ref[0] if side == 0 else 1 - place_ref[0]

    def copies(t):
        slot = lax.rem(t, 2)
        cols = pl.ds(pl.multiple_of(t * TILE, TILE), TILE)
        own_cols = pl.ds(pl.multiple_of(half * COLS + t * TILE, TILE), TILE)
        pairs = [(own.at[:, own_cols], slots.at[slot, pl.ds(0, HD)])]
        for part, start in zip(parts, (HD, 2 * HD, 2 * HD + HALF, 3 * HD)):
            height = part.shape[0]
            pairs.append((part.at[:, cols], slots.at[slot, pl.ds(start, height)]))
        return [
            pltpu.make_async_copy(source, target, sems.at[slot, index])
            for index, (source, target) in enumerate(pairs)
        ]

    @pl.when(step == 0)
    def _():
        for copy in copies(step):
            copy.start()
        for d in range(4):
            every[:, d * HD : (d + 1) * HD] = rows[d][...]

    @pl.when(step + 1 < tiles)
    def _():
        for copy in copies(step + 1):
            copy.start()

    for copy in copies(step):
        copy.wait()
    total = nn(every[...], slots[lax.rem(step, 2)])
    keep_ref[...] = total[:TOK].astype(BF16)
    send_ref[...] = total[TOK:].astype(BF16)


def project(side, place, rows, own, parts):
    tiles = LONG // TILE
    out = pl.BlockSpec((TOK, TILE), lambda t, place_ref: (0, t))
    return pl.pallas_call(
        lambda *refs: project_body(side, *refs),
        grid_spec=pltpu.PrefetchScalarGridSpec(
            num_scalar_prefetch=1,
            grid=(tiles,),
            in_specs=[pl.BlockSpec((2 * TOK, HD), lambda t, place_ref: (0, 0))] * 4
            + [pl.BlockSpec(memory_space=pl.ANY)] * 5,
            out_specs=[out, out],
            scratch_shapes=[
                pltpu.VMEM((2 * TOK, 4 * HD), BF16),
                pltpu.VMEM((2, 4 * HD, TILE), BF16),
                pltpu.SemaphoreType.DMA((2, 5)),
            ],
        ),
        out_shape=[jax.ShapeDtypeStruct((TOK, LONG), BF16)] * 2,
        compiler_params=room(16),
        cost_estimate=cost(2 * 256 * 2560 * LONG, 2560 * LONG * 2),
        name="project",
    )(place, *rows, own, *parts)


def pair_kernel(place_ref, *refs):
    rows, got_ref, own, cross, cross_other = refs[:4], refs[4], refs[5], refs[6], refs[7]
    outs, (every, held, sems) = refs[8:12], refs[12:]
    copies = []
    for side, part in enumerate((cross, cross_other)):
        half = place_ref[0] if side == 0 else 1 - place_ref[0]
        cols = pl.ds(pl.multiple_of(half * COLS + LONG, 512), WIDTH)
        copies.append(
            pltpu.make_async_copy(own.at[:, cols], held.at[side, pl.ds(0, HD)], sems.at[side, 0])
        )
        copies.append(pltpu.make_async_copy(part, held.at[side, pl.ds(HD, HD)], sems.at[side, 1]))
    for copy in copies:
        copy.start()
    for d in range(4):
        every[d * TOK : (d + 1) * TOK, :HD] = rows[d][:TOK, :]
    every[:, HD:] = got_ref[...]
    for copy in copies:
        copy.wait()

    def tile(index, carry):
        side, t = index // 2, lax.rem(index, 2)
        cols = pl.ds(pl.multiple_of(t * 512, 512), 512)
        total = nn(every[...], held[side, :, cols]).astype(BF16)
        out_cols = pl.ds(pl.multiple_of(index * 512, 512), 512)
        for d in range(4):
            outs[d][:, out_cols] = total[d * TOK : (d + 1) * TOK]
        return carry

    lax.fori_loop(0, 4, tile, 0)


def pair_project(place, rows, got, own, cross, cross_other):
    return pl.pallas_call(
        pair_kernel,
        in_specs=[SMEM] + [VMEM] * 5 + [pl.BlockSpec(memory_space=pl.ANY)] * 3,
        out_specs=[VMEM] * 4,
        out_shape=[jax.ShapeDtypeStruct((TOK, 2 * WIDTH), BF16)] * 4,
        scratch_shapes=[
            pltpu.VMEM((4 * TOK, 2 * HD), BF16),
            pltpu.VMEM((2, 2 * HD, WIDTH), BF16),
            pltpu.SemaphoreType.DMA((2, 2)),
        ],
        compiler_params=room(16),
        cost_estimate=cost(2 * 256 * 1280 * 2 * WIDTH, 1280 * 2 * WIDTH * 2),
        name="pair_project",
    )(place, *rows, got, own, cross, cross_other)


def finish_kernel(place_ref, *refs):
    parts, out_ref = refs[:8], refs[-1]
    for side in range(2):
        half = place_ref[0] if side == 0 else 1 - place_ref[0]
        start = half * COLS
        total = parts[2 * side][...].astype(F32) + parts[2 * side + 1][...].astype(F32)
        out_ref[0, :, pl.ds(pl.multiple_of(start, 512), LONG)] = total.astype(BF16)
        cols = slice(side * WIDTH, (side + 1) * WIDTH)
        total = parts[4][:, cols].astype(F32)
        for part in parts[5:8]:
            total = total + part[:, cols].astype(F32)
        out_ref[0, :, pl.ds(pl.multiple_of(start + LONG, 512), WIDTH)] = total.astype(BF16)


def finish(block, place, parts, held=None):
    held = [] if held is None else [held]
    whole = [pl.BlockSpec(part.shape, lambda i: (0, 0)) for part in parts]
    return pl.pallas_call(
        finish_kernel,
        grid=(1,),
        in_specs=[SMEM] + whole + [pl.BlockSpec(memory_space=pl.ANY)] * len(held),
        out_specs=pl.BlockSpec((1, TOK, WIDE), lambda i: (block, 0, 0)),
        out_shape=jax.ShapeDtypeStruct((2, TOK, WIDE), BF16),
        input_output_aliases={9: 0} if held else {},
        compiler_params=room(16),
        cost_estimate=cost(1 << 20, 3 << 20),
        name="finish",
    )(place, *parts, *held)


def per_device(queries, keys, values, rates, gate_fast, up_fast, down_fast, out_gain, out_proj):
    core = lax.axis_index("core")
    place = jnp.stack([core] + [lax.axis_index(name) for name in ("x", "z", "yl")])
    place = place.astype(jnp.int32)
    gain = out_gain.reshape(1, HD)
    rates = rates.transpose(0, 2, 1)

    first = to_heads(pack_first(keys, values, rates))
    first_far = shift(first, "core", 1, 2)
    second = to_heads(pack_second(keys, values, rates, queries))
    second_far = shift(second, "core", 1, 2)

    mine = lax.dynamic_slice(out_proj, (0, core * COLS), (HD, LONG))
    slab = lax.dynamic_slice(out_proj, (0, core * COLS + LONG), (HD, WIDTH))
    cross = shift(slab, "yl", 1, 2)
    cross_other = shift(cross, "core", 1, 2)
    before = shift(mine, "z", 1, 4)
    after = shift(mine, "z", 3, 4)
    far_low = shift(before[:HALF], "z", 1, 4)
    far_high = shift(after[HALF:], "z", 3, 4)
    own_side = (before, far_low, far_high, after)
    other_before, other_after = (shift(part, "core", 1, 2) for part in (before, after))
    other_low, other_high = (shift(part, "core", 1, 2) for part in (far_low, far_high))
    other_side = (other_before, other_low, other_high, other_after)

    halves = start_half(place, gate_fast, up_fast, down_fast)
    master, row_norm, col_norm = start_full(gate_fast, up_fast, down_fast)

    def spread(block, weights):
        *rows, trade = apply_weights(block, place, weights, gain, second)
        got = shift(trade, "yl", 1, 2)
        back = {d: shift(rows[d], "z", 4 - d, 4) for d in (2, 1, 3)}
        mine, *others = pair_project(place, rows, got, out_proj, cross, cross_other)
        returned = {d: shift(others[d - 1], "z", 4 - d, 4) for d in (2, 1, 3)}
        ordered = [rows[0], back[3], back[2], back[1]]
        parts = []
        for side, gathered in enumerate((own_side, other_side)):
            keep, send = project(side, place, ordered, out_proj, gathered)
            parts += [keep, shift(send, "yl", 1, 2)]
        return parts + [mine] + [returned[d] for d in (1, 2, 3)]

    total = sum_over_ctx(grads(place, halves, first, first_far))
    weights = renorm(place, [master], row_norm, col_norm, total)
    parts = grads(place, weights, second, second_far)
    total = sum_over_ctx(parts)
    parts = spread(0, weights)
    out = finish(0, place, parts)
    weights = renorm(place, weights, row_norm, col_norm, total, True)
    return finish(1, place, spread(1, weights), out)


def solution(mesh):
    fine = Mesh(mesh.devices.reshape(SIZES), AXES)
    tokens = P(None, AXES, None)
    head = ("z", "yl")
    placed = (
        tokens,
        tokens,
        tokens,
        tokens,
        P(head, None, None),
        P(head, None, None),
        P(head, None, None),
        P(head),
        P(head, None),
    )
    return jax.shard_map(per_device, mesh=fine, in_specs=placed, out_specs=tokens, check_vma=False)
```

```python
import jax
import jax.numpy as jnp
from jax import lax
from jax.experimental import pallas as pl
from jax.experimental.pallas import tpu as pltpu
from jax.sharding import Mesh, PartitionSpec as P

F32 = jnp.float32
BF16 = jnp.bfloat16
AXES = ("x", "yh", "core", "z", "yl")
SIZES = (4, 2, 2, 4, 2)
HD = 640
WIDE = 5120
TOK = 64
HALF = 320
PART = 80
PIECE = 240
COLS = 2560
LONG = 1536
WIDTH = 1024
TILE = 512


VMEM = pl.BlockSpec(memory_space=pltpu.VMEM)
SMEM = pl.BlockSpec(memory_space=pltpu.SMEM)


def cost(flops, moved):
    return pl.CostEstimate(flops=flops, bytes_accessed=moved, transcendentals=0)


def room(mib):
    return pltpu.CompilerParams(vmem_limit_bytes=mib << 20)


def nt(left, right):
    return lax.dot_general(left, right, (((1,), (1,)), ((), ())), preferred_element_type=F32)


def nn(left, right):
    return lax.dot_general(left, right, (((1,), (0,)), ((), ())), preferred_element_type=F32)


def shift(array, axis, by, size):
    return lax.ppermute(array, axis, [(i, (i + by) % size) for i in range(size)])


def to_heads(array):
    return lax.all_to_all(array, ("z", "yl"), 0, 0, tiled=True)


def add(*terms):
    total = terms[0].astype(F32)
    for term in terms[1:]:
        total = total + term.astype(F32)
    return total


def split(matrix):
    high = matrix.astype(BF16)
    return high, (matrix - high.astype(F32)).astype(BF16)


def pack_keys(key_block, value_block, rate_block, out_ref):
    rates = rate_block[0].astype(F32)
    row = lax.broadcasted_iota(jnp.int32, (TOK, TOK), 0)
    lane = lax.broadcasted_iota(jnp.int32, (TOK, TOK), 1)
    for head in range(8):
        cols = slice(head * HD, (head + 1) * HD)
        out_ref[head, :TOK, :] = key_block[0, :, cols]
        spread = jnp.broadcast_to(rates[head : head + 1, :], (TOK, TOK))
        rate = jnp.sum(jnp.where(row == lane, spread, 0.0), axis=1, keepdims=True)
        target = value_block[0, :, cols].astype(F32) * rate
        out_ref[head, TOK : 2 * TOK, :] = target.astype(BF16)


def pack_first_kernel(key_ref, value_ref, rate_ref, out_ref):
    pack_keys(key_ref, value_ref, rate_ref, out_ref)


def pack_second_kernel(key_ref, value_ref, rate_ref, query_ref, out_ref):
    pack_keys(key_ref, value_ref, rate_ref, out_ref)
    for head in range(8):
        for block in range(2):
            start = (2 + block) * TOK
            cols = slice(head * HD, (head + 1) * HD)
            out_ref[head, start : start + TOK, :] = query_ref[block, :, cols]


def block_of(block, width):
    return pl.BlockSpec((1, TOK, width), lambda i: (block, 0, 0))


def rates_of(block):
    return pl.BlockSpec((1, 8, TOK), lambda i: (block, 0, 0))


def pack_first(keys, values, rates):
    return pl.pallas_call(
        pack_first_kernel,
        grid=(1,),
        in_specs=[block_of(0, WIDE), block_of(0, WIDE), rates_of(0)],
        out_specs=pl.BlockSpec((8, 2 * TOK, HD), lambda i: (0, 0, 0)),
        out_shape=jax.ShapeDtypeStruct((8, 2 * TOK, HD), BF16),
        cost_estimate=cost(1 << 20, 4 * TOK * WIDE * 2),
        name="pack_first",
    )(keys, values, rates)


def pack_second(keys, values, rates, queries):
    return pl.pallas_call(
        pack_second_kernel,
        grid=(1,),
        in_specs=[
            block_of(1, WIDE),
            block_of(1, WIDE),
            rates_of(1),
            pl.BlockSpec((2, TOK, WIDE), lambda i: (0, 0, 0)),
        ],
        out_specs=pl.BlockSpec((8, 4 * TOK, HD), lambda i: (0, 0, 0)),
        out_shape=jax.ShapeDtypeStruct((8, 4 * TOK, HD), BF16),
        cost_estimate=cost(1 << 20, 8 * TOK * WIDE * 2),
        name="pack_second",
    )(keys, values, rates, queries)


def start_half_kernel(place_ref, gate_ref, up_ref, down_ref, high_ref, low_ref, loaded, turned, sems):
    core = place_ref[0]
    half = pl.ds(pl.multiple_of(core * HALF, HALF), HALF)
    tiles = pl.ds(pl.multiple_of(core * 256, 256), 384)
    inside = pl.ds(pl.multiple_of(core * (HALF - 256), 64), HALF)
    copies = [
        pltpu.make_async_copy(gate_ref.at[0, :, tiles], loaded.at[0], sems.at[0]),
        pltpu.make_async_copy(up_ref.at[0, :, tiles], loaded.at[1], sems.at[1]),
        pltpu.make_async_copy(down_ref.at[0, half], turned.at[pl.ds(384, HALF)], sems.at[2]),
    ]
    for copy in copies:
        copy.start()
    for slot in range(2):
        copies[slot].wait()
        turned[:384, :] = loaded[slot].T
        high_ref[slot], low_ref[slot] = split(turned[inside, :])
    copies[2].wait()
    high_ref[2], low_ref[2] = split(turned[384:, :])


def start_half(place, gate, up, down):
    return pl.pallas_call(
        start_half_kernel,
        in_specs=[SMEM] + [pl.BlockSpec(memory_space=pltpu.HBM)] * 3,
        out_specs=[VMEM] * 2,
        out_shape=[jax.ShapeDtypeStruct((3, HALF, HD), BF16)] * 2,
        scratch_shapes=[
            pltpu.VMEM((2, HD, 384), F32),
            pltpu.VMEM((384 + HALF, HD), F32),
            pltpu.SemaphoreType.DMA((3,)),
        ],
        compiler_params=room(16),
        cost_estimate=cost(1 << 24, 3 * HD * HD * 6),
        name="start_half",
    )(place, gate, up, down)


def start_full_kernel(gate_ref, up_ref, down_ref, master_ref, row_norm_ref, col_norm_ref):
    for slot, ref in ((0, gate_ref), (1, up_ref)):
        matrix = ref[0].T
        master_ref[slot] = matrix
        row_norm_ref[slot] = jnp.sqrt(jnp.sum(matrix * matrix, axis=1, keepdims=True))
    matrix = down_ref[0]
    master_ref[2] = matrix
    col_norm_ref[...] = jnp.sqrt(jnp.sum(matrix * matrix, axis=0, keepdims=True))


def start_full(gate, up, down):
    return pl.pallas_call(
        start_full_kernel,
        in_specs=[VMEM] * 3,
        out_specs=[VMEM] * 3,
        out_shape=[
            pltpu.VMEM((3, HD, HD), F32),
            pltpu.VMEM((2, HD, 1), F32),
            pltpu.VMEM((1, HD), F32),
        ],
        compiler_params=room(16),
        cost_estimate=cost(1 << 24, 3 * HD * HD * 8),
        name="start_full",
    )(gate, up, down)


def renorm_kernel(count, place_ref, *refs):
    old_refs, (row_norm_ref, col_norm_ref) = refs[:count], refs[count : count + 2]
    pieces, outs, down_ref = refs[count + 2 : count + 10], refs[count + 10 : -1], refs[-1]
    core, x = place_ref[0], place_ref[1]
    squares = jnp.zeros((8, HD), F32)

    def store(where, matrix):
        for out, part in zip(outs, split(matrix)):
            out[where] = part

    def moved_rows(slot, rows, step):
        total = step.astype(F32)
        for old_ref in old_refs:
            total = total + old_ref[slot, rows, :].astype(F32)
        return total

    for index, piece in enumerate(pieces):
        side, d = index // 4, index % 4
        owner = core if side == 0 else 1 - core
        start = pl.multiple_of(owner * HALF + lax.rem(x + 4 - d, 4) * PART, 16)
        rows = pl.ds(start, PART)
        for slot in range(2):
            moved = moved_rows(slot, rows, piece[slot * PART : (slot + 1) * PART, :])
            scale = row_norm_ref[slot, rows, :] * lax.rsqrt(
                jnp.sum(moved * moved, axis=1, keepdims=True) + 1e-6
            )
            store((slot, rows, slice(None)), moved * scale)
        moved = moved_rows(2, rows, piece[2 * PART :, :])
        down_ref[rows, :] = moved
        squares = squares + jnp.sum((moved * moved).reshape(PART // 8, 8, HD), axis=0)
    scale = col_norm_ref[...] * lax.rsqrt(jnp.sum(squares, axis=0, keepdims=True) + 1e-6)
    store(2, down_ref[...] * scale)


def renorm(place, weights, row_norm, col_norm, pieces, last=False):
    return pl.pallas_call(
        lambda *refs: renorm_kernel(len(weights), *refs),
        in_specs=[SMEM] + [VMEM] * (10 + len(weights)),
        out_specs=[VMEM] * (1 if last else 2),
        out_shape=[pltpu.VMEM((3, HD, HD), BF16)] * (1 if last else 2),
        scratch_shapes=[pltpu.VMEM((HD, HD), F32)],
        compiler_params=room(16),
        cost_estimate=cost(1 << 24, 3 * HD * HD * 10),
        name="renorm",
    )(place, *weights, row_norm, col_norm, *pieces)


def grads_kernel(place_ref, high_ref, low_ref, near_ref, far_ref, *refs):
    outs, (inner, total), loaded = refs[:4], refs[4:6], refs[6:]
    core, x = place_ref[0], place_ref[1]
    copies = []
    if loaded:
        held, sems = loaded
        copies = [
            pltpu.make_async_copy(ref, held.at[index], sems.at[index])
            for index, ref in enumerate((high_ref, low_ref))
        ]
        high_ref, low_ref = held.at[0], held.at[1]
    for copy in copies:
        copy.start()
    for copy in copies:
        copy.wait()
    height = high_ref.shape[1]
    half = pl.ds(pl.multiple_of(core * (height - HALF), HALF), HALF)

    def product(slot, rows):
        return nt(high_ref[slot, half, :], rows) + nt(low_ref[slot, half, :], rows)

    for side, ref in enumerate((near_ref, far_ref)):

        def chunk(step, carry, side=side, ref=ref):
            four = pl.ds(step * 4, 4)
            rows = pl.ds(pl.multiple_of(side * 512 + step * 256, 256), 256)
            key = ref[four, :TOK, :].reshape(4 * TOK, HD)
            gate = product(0, key)
            up = product(1, key)
            back = product(2, ref[four, TOK : 2 * TOK, :].reshape(4 * TOK, HD))
            sigma = jax.nn.sigmoid(gate)
            silu = gate * sigma
            inner[0, :, rows] = (back * up * sigma * (1.0 + gate * (1.0 - sigma))).astype(BF16)
            inner[1, :, rows] = (back * silu).astype(BF16)
            inner[2, :, rows] = (silu * up).astype(BF16)
            return carry

        lax.fori_loop(0, 2, chunk, 0)

    def finish(slot, carry):
        kind = pl.ds(pl.multiple_of(slot // 2 * TOK, TOK), TOK)
        near = nn(inner[slot, :, :512], near_ref[:, kind, :].reshape(8 * TOK, HD))
        far = nn(inner[slot, :, 512:], far_ref[:, kind, :].reshape(8 * TOK, HD))
        total[slot] = near + far
        return carry

    lax.fori_loop(0, 3, finish, 0)
    for d in range(4):
        rows = pl.ds(pl.multiple_of(lax.rem(x + d, 4) * PART, 16), PART)
        for slot in range(3):
            outs[d][slot * PART : (slot + 1) * PART, :] = total[slot, rows, :].astype(outs[d].dtype)


def grads(place, weights, near, far):
    part = pl.BlockSpec((8, 2 * TOK, HD), lambda i: (0, 0, 0))
    held = pl.BlockSpec(weights[0].shape, lambda i: (0, 0, 0))
    extra = []
    if weights[0].shape[1] == HALF:
        held = pl.BlockSpec(memory_space=pltpu.HBM)
        extra = [pltpu.VMEM((2, 3, HALF, HD), BF16), pltpu.SemaphoreType.DMA((2,))]
    return pl.pallas_call(
        grads_kernel,
        grid=(1,),
        in_specs=[SMEM] + [held] * 2 + [part] * 2,
        out_specs=[pl.BlockSpec((PIECE, HD), lambda i: (0, 0))] * 4,
        out_shape=[pltpu.VMEM((PIECE, HD), F32 if d == 0 else BF16) for d in range(4)],
        scratch_shapes=[
            pltpu.VMEM((3, HALF, 16 * TOK), BF16),
            pltpu.VMEM((3, HALF, HD), F32),
        ]
        + extra,
        cost_estimate=cost(12 * 16 * TOK * HALF * HD, 8 << 20),
        compiler_params=None if extra else room(20),
        name="grads",
    )(place, *weights, near, far)


def sum_over_ctx(parts):
    received = {d: shift(parts[d], "x", d, 4) for d in (1, 3, 2)}
    mine = lax.optimization_barrier(add(parts[0], received[1], received[3], received[2]))
    other = shift(mine.astype(BF16), "yh", 1, 2)
    mine = add(mine, other).astype(BF16)
    near = {d: shift(mine, "x", d, 4) for d in (1, 3, 2)}
    pieces = [mine, near[1], near[2], near[3]]
    far = {d: shift(pieces[d], "core", 1, 2) for d in (0, 1, 3, 2)}
    return pieces + [far[d] for d in range(4)]


def apply_kernel(place_ref, high_ref, gain_ref, query_ref, *refs):
    outs, trade_ref, (rows_in, rows_out) = refs[:4], refs[4], refs[5:]
    z, yl = place_ref[2], place_ref[3]
    for d in range(4):
        for dy in range(2):
            source = lax.rem(z + 4 - d, 4) * 2 + lax.rem(yl + dy, 2)
            rows_in[pl.ds((d * 2 + dy) * TOK, TOK), :] = query_ref[source]
    gain = gain_ref[...]

    def chunk(step, carry):
        rows = pl.ds(pl.multiple_of(step * 4 * TOK, 4 * TOK), 4 * TOK)
        query = rows_in[rows, :]
        gate = nt(query, high_ref[0])
        up = nt(query, high_ref[1])
        hidden = (gate * jax.nn.sigmoid(gate) * up).astype(BF16)
        out = nn(hidden, high_ref[2])
        mean = jnp.sum(out * out, axis=1, keepdims=True) * (1.0 / HD)
        rows_out[rows, :] = (out * lax.rsqrt(mean + 1e-5) * gain).astype(BF16)
        return carry

    lax.fori_loop(0, 2, chunk, 0)
    for d in range(4):
        outs[d][...] = rows_out[d * 2 * TOK : (d + 1) * 2 * TOK, :]
        trade_ref[d * TOK : (d + 1) * TOK, :] = rows_out[(2 * d + 1) * TOK : (2 * d + 2) * TOK, :]


def apply_weights(block, place, weights, gain, queries):
    return pl.pallas_call(
        apply_kernel,
        grid=(1,),
        in_specs=[
            SMEM,
            pl.BlockSpec((3, HD, HD), lambda i: (0, 0, 0)),
            pl.BlockSpec((1, HD), lambda i: (0, 0)),
            pl.BlockSpec((8, TOK, HD), lambda i: (0, 2 + block, 0)),
        ],
        out_specs=[pl.BlockSpec((2 * TOK, HD), lambda i: (0, 0))] * 4
        + [pl.BlockSpec((4 * TOK, HD), lambda i: (0, 0))],
        out_shape=[jax.ShapeDtypeStruct((2 * TOK, HD), BF16)] * 4
        + [jax.ShapeDtypeStruct((4 * TOK, HD), BF16)],
        scratch_shapes=[pltpu.VMEM((8 * TOK, HD), BF16)] * 2,
        compiler_params=room(16),
        cost_estimate=cost(6 * 8 * TOK * HD * HD, 5 << 20),
        name="apply_weights",
    )(place, weights[0], gain, queries)


def project_body(side, place_ref, *refs):
    rows, own, parts = refs[:4], refs[4], refs[5:9]
    keep_ref, send_ref, every, slots, sems = refs[9:]
    step = pl.program_id(0)
    tiles = LONG // TILE
    half = place_ref[0] if side == 0 else 1 - place_ref[0]

    def copies(t):
        slot = lax.rem(t, 2)
        cols = pl.ds(pl.multiple_of(t * TILE, TILE), TILE)
        own_cols = pl.ds(pl.multiple_of(half * COLS + t * TILE, TILE), TILE)
        pairs = [(own.at[:, own_cols], slots.at[slot, pl.ds(0, HD)])]
        for part, start in zip(parts, (HD, 2 * HD, 2 * HD + HALF, 3 * HD)):
            height = part.shape[0]
            pairs.append((part.at[:, cols], slots.at[slot, pl.ds(start, height)]))
        return [
            pltpu.make_async_copy(source, target, sems.at[slot, index])
            for index, (source, target) in enumerate(pairs)
        ]

    @pl.when(step == 0)
    def _():
        for copy in copies(step):
            copy.start()
        for d in range(4):
            every[:, d * HD : (d + 1) * HD] = rows[d][...]

    @pl.when(step + 1 < tiles)
    def _():
        for copy in copies(step + 1):
            copy.start()

    for copy in copies(step):
        copy.wait()
    total = nn(every[...], slots[lax.rem(step, 2)])
    keep_ref[...] = total[:TOK].astype(BF16)
    send_ref[...] = total[TOK:].astype(BF16)


def project(side, place, rows, own, parts):
    tiles = LONG // TILE
    out = pl.BlockSpec((TOK, TILE), lambda t, place_ref: (0, t))
    return pl.pallas_call(
        lambda *refs: project_body(side, *refs),
        grid_spec=pltpu.PrefetchScalarGridSpec(
            num_scalar_prefetch=1,
            grid=(tiles,),
            in_specs=[pl.BlockSpec((2 * TOK, HD), lambda t, place_ref: (0, 0))] * 4
            + [pl.BlockSpec(memory_space=pl.ANY)] * 5,
            out_specs=[out, out],
            scratch_shapes=[
                pltpu.VMEM((2 * TOK, 4 * HD), BF16),
                pltpu.VMEM((2, 4 * HD, TILE), BF16),
                pltpu.SemaphoreType.DMA((2, 5)),
            ],
        ),
        out_shape=[jax.ShapeDtypeStruct((TOK, LONG), BF16)] * 2,
        compiler_params=room(16),
        cost_estimate=cost(2 * 256 * 2560 * LONG, 2560 * LONG * 2),
        name="project",
    )(place, *rows, own, *parts)


def pair_kernel(place_ref, *refs):
    rows, got_ref, own, cross, cross_other = refs[:4], refs[4], refs[5], refs[6], refs[7]
    outs, (every, held, sems) = refs[8:12], refs[12:]
    copies = []
    for side, part in enumerate((cross, cross_other)):
        half = place_ref[0] if side == 0 else 1 - place_ref[0]
        cols = pl.ds(pl.multiple_of(half * COLS + LONG, 512), WIDTH)
        copies.append(
            pltpu.make_async_copy(own.at[:, cols], held.at[side, pl.ds(0, HD)], sems.at[side, 0])
        )
        copies.append(pltpu.make_async_copy(part, held.at[side, pl.ds(HD, HD)], sems.at[side, 1]))
    for copy in copies:
        copy.start()
    for d in range(4):
        every[d * TOK : (d + 1) * TOK, :HD] = rows[d][:TOK, :]
    every[:, HD:] = got_ref[...]
    for copy in copies:
        copy.wait()

    def tile(index, carry):
        side, t = index // 2, lax.rem(index, 2)
        cols = pl.ds(pl.multiple_of(t * 512, 512), 512)
        total = nn(every[...], held[side, :, cols]).astype(BF16)
        out_cols = pl.ds(pl.multiple_of(index * 512, 512), 512)
        for d in range(4):
            outs[d][:, out_cols] = total[d * TOK : (d + 1) * TOK]
        return carry

    lax.fori_loop(0, 4, tile, 0)


def pair_project(place, rows, got, own, cross, cross_other):
    return pl.pallas_call(
        pair_kernel,
        in_specs=[SMEM] + [VMEM] * 5 + [pl.BlockSpec(memory_space=pl.ANY)] * 3,
        out_specs=[VMEM] * 4,
        out_shape=[jax.ShapeDtypeStruct((TOK, 2 * WIDTH), BF16)] * 4,
        scratch_shapes=[
            pltpu.VMEM((4 * TOK, 2 * HD), BF16),
            pltpu.VMEM((2, 2 * HD, WIDTH), BF16),
            pltpu.SemaphoreType.DMA((2, 2)),
        ],
        compiler_params=room(16),
        cost_estimate=cost(2 * 256 * 1280 * 2 * WIDTH, 1280 * 2 * WIDTH * 2),
        name="pair_project",
    )(place, *rows, got, own, cross, cross_other)


def finish_kernel(sides, place_ref, *refs):
    out_ref = refs[-1]
    parts = refs[: 2 * sides + 4]
    for side in range(2):
        half = place_ref[0] if side == 0 else 1 - place_ref[0]
        start = half * COLS
        if side < sides:
            total = parts[2 * side][...].astype(F32) + parts[2 * side + 1][...].astype(F32)
            out_ref[0, :, pl.ds(pl.multiple_of(start, 512), LONG)] = total.astype(BF16)
        cols = slice(side * WIDTH, (side + 1) * WIDTH)
        total = parts[2 * sides][:, cols].astype(F32)
        for part in parts[2 * sides + 1 :]:
            total = total + part[:, cols].astype(F32)
        out_ref[0, :, pl.ds(pl.multiple_of(start + LONG, 512), WIDTH)] = total.astype(BF16)


def finish(block, place, parts, held=None):
    held = [] if held is None else [held]
    whole = [pl.BlockSpec(part.shape, lambda i: (0, 0)) for part in parts]
    sides = (len(parts) - 4) // 2
    return pl.pallas_call(
        lambda *refs: finish_kernel(sides, *refs),
        grid=(1,),
        in_specs=[SMEM] + whole + [pl.BlockSpec(memory_space=pl.ANY)] * len(held),
        out_specs=pl.BlockSpec((1, TOK, WIDE), lambda i: (block, 0, 0)),
        out_shape=jax.ShapeDtypeStruct((2, TOK, WIDE), BF16),
        input_output_aliases={1 + len(parts): 0} if held else {},
        compiler_params=room(16),
        cost_estimate=cost(1 << 20, 3 << 20),
        name="finish",
    )(place, *parts, *held)


def finish_last_kernel(place_ref, keep_ref, got_ref, held_ref, out_ref, total, sem):
    start = (1 - place_ref[0]) * COLS
    total[...] = (keep_ref[...].astype(F32) + got_ref[...].astype(F32)).astype(BF16)
    cols = pl.ds(pl.multiple_of(start, 512), LONG)
    copy = pltpu.make_async_copy(total, out_ref.at[1, :, cols], sem)
    copy.start()
    copy.wait()


def finish_last(place, keep, got, held):
    return pl.pallas_call(
        finish_last_kernel,
        in_specs=[SMEM, VMEM, VMEM, pl.BlockSpec(memory_space=pl.ANY)],
        out_specs=pl.BlockSpec(memory_space=pl.ANY),
        out_shape=jax.ShapeDtypeStruct((2, TOK, WIDE), BF16),
        scratch_shapes=[pltpu.VMEM((TOK, LONG), BF16), pltpu.SemaphoreType.DMA(())],
        input_output_aliases={3: 0},
        compiler_params=room(16),
        cost_estimate=cost(1 << 18, 1 << 19),
        name="finish_last",
    )(place, keep, got, held)


def per_device(queries, keys, values, rates, gate_fast, up_fast, down_fast, out_gain, out_proj):
    core = lax.axis_index("core")
    place = jnp.stack([core] + [lax.axis_index(name) for name in ("x", "z", "yl")])
    place = place.astype(jnp.int32)
    gain = out_gain.reshape(1, HD)
    rates = rates.transpose(0, 2, 1)

    first = to_heads(pack_first(keys, values, rates))
    first_far = shift(first, "core", 1, 2)
    second = to_heads(pack_second(keys, values, rates, queries))
    second_far = shift(second, "core", 1, 2)

    mine = lax.dynamic_slice(out_proj, (0, core * COLS), (HD, LONG))
    slab = lax.dynamic_slice(out_proj, (0, core * COLS + LONG), (HD, WIDTH))
    cross = shift(slab, "yl", 1, 2)
    cross_other = shift(cross, "core", 1, 2)
    before = shift(mine, "z", 1, 4)
    after = shift(mine, "z", 3, 4)
    far_low = shift(before[:HALF], "z", 1, 4)
    far_high = shift(after[HALF:], "z", 3, 4)
    own_side = (before, far_low, far_high, after)
    other_before, other_after = (shift(part, "core", 1, 2) for part in (before, after))
    other_low, other_high = (shift(part, "core", 1, 2) for part in (far_low, far_high))
    other_side = (other_before, other_low, other_high, other_after)

    halves = start_half(place, gate_fast, up_fast, down_fast)
    master, row_norm, col_norm = start_full(gate_fast, up_fast, down_fast)

    def spread(block, weights):
        *rows, trade = apply_weights(block, place, weights, gain, second)
        got = shift(trade, "yl", 1, 2)
        back = {d: shift(rows[d], "z", 4 - d, 4) for d in (2, 1, 3)}
        mine, *others = pair_project(place, rows, got, out_proj, cross, cross_other)
        returned = {d: shift(others[d - 1], "z", 4 - d, 4) for d in (2, 1, 3)}
        ordered = [rows[0], back[3], back[2], back[1]]
        parts = []
        for side, gathered in enumerate((own_side, other_side)):
            keep, send = project(side, place, ordered, out_proj, gathered)
            parts += [keep, shift(send, "yl", 1, 2)]
        return parts + [mine] + [returned[d] for d in (1, 2, 3)]

    total = sum_over_ctx(grads(place, halves, first, first_far))
    weights = renorm(place, [master], row_norm, col_norm, total)
    parts = grads(place, weights, second, second_far)
    total = sum_over_ctx(parts)
    parts = spread(0, weights)
    out = finish(0, place, parts)
    weights = renorm(place, weights, row_norm, col_norm, total, True)
    parts = spread(1, weights)
    out = finish(1, place, parts[:2] + parts[4:], out)
    return finish_last(place, parts[2], parts[3], out)


def solution(mesh):
    fine = Mesh(mesh.devices.reshape(SIZES), AXES)
    tokens = P(None, AXES, None)
    head = ("z", "yl")
    placed = (
        tokens,
        tokens,
        tokens,
        tokens,
        P(head, None, None),
        P(head, None, None),
        P(head, None, None),
        P(head),
        P(head, None),
    )
    return jax.shard_map(per_device, mesh=fine, in_specs=placed, out_specs=tokens, check_vma=False)
```
